128 devices in a mesh: req: 64 (over z, y, x), seq: 2 (over core).
Axes of the slice: x: 4, y: 4, z: 4, core: 2. Of those that a mesh axis runs over, the one named last changes fastest.
Arguments:
- tokens: bfloat16 [16384, 1536], P(('req', 'seq')), may hold values from -6 to 6
- attn_gain: float32 [1536], replicated, may hold values from 0.5 to 1.5
- w_qkv: bfloat16 [1536, 2560], replicated, may hold values from -80 to 80
- w_out: bfloat16 [1536, 1536], replicated, may hold values from -0.15625 to 0.15625
- k_cache: bfloat16 [64, 2048, 512], P('req', 'seq'), may hold values from -6 to 6
- v_cache: bfloat16 [64, 2048, 512], P('req', 'seq'), may hold values from -7.5 to 7.5
- cache_len: int32 [64], P('req'), may hold values from 1 to 2048, as said below
- ffn_gain: float32 [1536], replicated, may hold values from 0.5 to 1.5
- routes: int32 [16384, 8], P(('req', 'seq')), may hold values from 0 to 39, as said below
- route_scores: float32 [16384, 8], P(('req', 'seq')), may hold values from 0.05 to 1
- replica_slot: int32 [16384, 40], P(('req', 'seq')), may hold values from 0 to 127, as said below
- expert_up: bfloat16 [128, 1536, 1024], P(('req', 'seq')), may hold values from -2 to 2, as said below
- expert_down: bfloat16 [128, 512, 1536], P(('req', 'seq')), may hold values from -2 to 2, as said below
Outputs:
- attended: bfloat16 [16384, 1536], P(('req', 'seq'))
- stream: bfloat16 [16384, 1536], P(('req', 'seq'))
- expert_mix: bfloat16 [16384, 1536], P(('req', 'seq'))
- appended: bfloat16 [16384, 1024], P(('req', 'seq'))
The draws below stay inside these ranges and needn't reach their ends.
Inputs may be any that keep to these rules, and one draw needn't show every extreme that they name: `routes`: each token names 8 different experts. Each slot hosts one expert, every expert at least one slot; replica_slot[t, e] is a slot hosting expert e. The 128 rows of one device (rows d * 128 to (d + 1) * 128 - 1) send at most 16 of their routes to any one slot (slot replica_slot[t, routes[t, k]]), and each device sends exactly 16 to some slot. `expert_up`: slots hosting the same expert hold equal weights. `expert_down`: slots hosting the same expert hold equal weights. `cache_len`: at least one request has exactly 2048 cached positions.
All inputs are finite; a program needn't handle non-finite values.
Results may differ from the reference program's by a relative error of at most 0.01.
Values may be sent and summed in bfloat16 or wider, within the bound.
A program may use at most 128 MiB of HBM per device.

```python
import math
import jax
import jax.numpy as jnp
from jax import lax

D = 1536
HEADS = 24
KV_HEADS = 8
HEAD = 64
EXPERTS = 40
FF = 512
TOP = 8
KEY_BLOCK = 128
SPAN_DEV = 128
SPAN = 256
CACHE = 2048
REQS = 64
TOKENS = 16384
SLOTS = 128
CAP = 16
N_REQ = 64
N_SEQ = 2


def slot_hosts(key):
    route_order = jax.random.permutation(jax.random.fold_in(key, 101), SLOTS).astype(jnp.int32)
    hosted = jnp.zeros((SLOTS,), jnp.int32).at[route_order].set(jnp.arange(SLOTS, dtype=jnp.int32) % EXPERTS)
    return (route_order, hosted)


def route_plan(key):
    route_order, hosted = slot_hosts(key)
    total = SPAN_DEV * TOP
    mean_load = (total + SLOTS - 1) // SLOTS
    sorted_slots = jnp.argsort(hosted * SLOTS + jnp.arange(SLOTS, dtype=jnp.int32)).astype(jnp.int32)

    def one_device(device):
        device_key = jax.random.fold_in(jax.random.fold_in(key, 141), device)
        visit = jax.random.permutation(jax.random.fold_in(device_key, 1), SLOTS).astype(jnp.int32)
        wanted = jax.random.randint(jax.random.fold_in(device_key, 2), (SLOTS,), mean_load, CAP + 1).astype(jnp.int32)
        wanted = wanted.at[0].set(CAP)
        before_load = jnp.cumsum(wanted).astype(jnp.int32) - wanted
        kept_load = jnp.clip(total - before_load, 0, wanted).astype(jnp.int32)
        load = jnp.zeros((SLOTS,), jnp.int32).at[visit].set(kept_load)
        ends = jnp.cumsum(load[sorted_slots]).astype(jnp.int32)
        entry = jnp.arange(total, dtype=jnp.int32)
        where_at = jnp.searchsorted(ends, entry, side='right').astype(jnp.int32)
        slot_rows = sorted_slots[where_at].reshape(TOP, SPAN_DEV).T
        shuffle = jax.random.permutation(jax.random.fold_in(device_key, 3), SPAN_DEV).astype(jnp.int32)
        return slot_rows[shuffle]
    chosen_slots = jax.vmap(one_device)(jnp.arange(N_REQ * N_SEQ, dtype=jnp.int32)).reshape(TOKENS, TOP)
    return (route_order, hosted, chosen_slots.astype(jnp.int32))


def draw_routes(key, part):
    route_order, hosted, chosen_slots = route_plan(key)
    return hosted[chosen_slots].astype(jnp.int32)


def draw_replica_slot(key, part):
    route_order, hosted, chosen_slots = route_plan(key)
    routes = hosted[chosen_slots].astype(jnp.int32)
    experts = jnp.arange(EXPERTS, dtype=jnp.int32)
    copies = (SLOTS - experts + EXPERTS - 1) // EXPERTS
    picked = jax.random.randint(jax.random.fold_in(key, 102), (TOKENS, EXPERTS), 0, 1 << 20) % copies[None, :]
    table = route_order[experts[None, :] + picked * EXPERTS].astype(jnp.int32)
    row_ids = jnp.arange(TOKENS, dtype=jnp.int32)[:, None]
    return table.at[row_ids, routes].set(chosen_slots).astype(jnp.int32)


def expert_table(key, salt_tag, row_count, col_count):
    route_order, hosted = slot_hosts(key)
    base_key = jax.random.fold_in(key, salt_tag)

    def draw_single(expert):
        expert_key = jax.random.fold_in(base_key, expert)
        return jnp.clip(jax.random.normal(expert_key, (row_count, col_count), jnp.float32), -6.0, 6.0)
    return jax.vmap(draw_single)(hosted) * row_count ** (-0.5)


def draw_expert_up(key, part):
    return expert_table(key, 103, D, 2 * FF).astype(jnp.bfloat16)


def draw_expert_down(key, part):
    return expert_table(key, 104, FF, D).astype(jnp.bfloat16)


def draw_w_qkv(key, part):
    col_count = (HEADS + 2 * KV_HEADS) * HEAD
    base_draw = jnp.clip(jax.random.normal(jax.random.fold_in(key, 111), (D, col_count), jnp.float32), -6.0, 6.0) * D ** (-0.5)
    return base_draw.astype(jnp.bfloat16)


def draw_cache_len(key, part):
    lengths = jax.random.randint(jax.random.fold_in(key, 121), (REQS,), 1, CACHE + 1)
    full_request = jax.random.randint(jax.random.fold_in(key, 122), (), 0, REQS)
    return jnp.where(jnp.arange(REQS) == full_request, CACHE, lengths).astype(jnp.int32)


def draw_v_cache(key, part):
    row_width = KV_HEADS * HEAD
    noise_part = jnp.clip(jax.random.normal(jax.random.fold_in(key, 131), (REQS, CACHE // 16, 16, row_width), jnp.float32), -6.0, 6.0)
    regions = jax.random.uniform(jax.random.fold_in(key, 132), (REQS, CACHE // 16, 1, row_width), jnp.float32, -1.5, 1.5)
    return (noise_part + regions).reshape(REQS, CACHE, row_width).astype(jnp.bfloat16)


def shard_levels(rng, dims, pieces, low, largest):
    loudness, own = 1.0, jax.random.fold_in(rng, 6)
    for axis_at, parts in pieces:
        steps = jnp.exp(jax.random.uniform(jax.random.fold_in(own, axis_at), (parts,), jnp.float32, low / len(pieces), largest / len(pieces)))
        loudness = loudness * jnp.repeat(steps, dims[axis_at] // parts).reshape([-1 if axis == axis_at else 1 for axis in range(len(dims))])
    return loudness


def centred(own_key, extent, scale, reach, split=(), held_as=jnp.bfloat16):
    entries = jax.random.normal(own_key, extent, jnp.float32) * scale
    if len(split) > 0:
        entries = shard_levels(own_key, extent, split, -0.22, 0.18) * entries
    return jnp.clip(entries, min=-reach, max=reach).astype(held_as)


def setup_inputs(seed: int = 0) -> dict:
    key_list = jax.random.split(jax.random.key(seed), 14)
    return {
        "tokens": centred(key_list[0], (TOKENS, D), 1.0, 6.0, ((0, 128),)),
        "attn_gain": jnp.clip(1.0 + 0.1 * jax.random.normal(key_list[1], (D,), jnp.float32), 0.5, 1.5),
        "w_qkv": draw_w_qkv(jax.random.fold_in(key_list[13], 71), 0),
        "w_out": centred(key_list[3], (HEADS * HEAD, D), (HEADS * HEAD) ** -0.5, 0.15625),
        "k_cache": centred(key_list[4], (REQS, CACHE, KV_HEADS * HEAD), 1.0, 6.0, ((0, 64), (1, 2))),
        "v_cache": draw_v_cache(jax.random.fold_in(key_list[13], 71), 0),
        "cache_len": draw_cache_len(jax.random.fold_in(key_list[13], 71), 0),
        "ffn_gain": jnp.clip(1.0 + 0.1 * jax.random.normal(key_list[7], (D,), jnp.float32), 0.5, 1.5),
        "routes": draw_routes(jax.random.fold_in(key_list[13], 71), 0),
        "route_scores": jnp.clip(jnp.exp(math.log(1.0) - 2.9957323 * jax.random.uniform(key_list[9], (TOKENS, TOP), jnp.float32) ** shard_levels(key_list[9], (TOKENS, TOP), ((0, 128),), -0.2, 0.2)), 0.05, 1.0),
        "replica_slot": draw_replica_slot(jax.random.fold_in(key_list[13], 71), 0),
        "expert_up": draw_expert_up(jax.random.fold_in(key_list[13], 71), 0),
        "expert_down": draw_expert_down(jax.random.fold_in(key_list[13], 71), 0),
    }


epsilon = 1e-06
residual_scale = 0.22
score_scale = 0.015625
rope_base = 10000.0
neg_big = -1e+30

def rms_scale(row_block, gain_vector):
    widened = row_block.astype(jnp.float32)
    mean_square = lax.optimization_barrier(jnp.mean(widened * widened, axis=-1, keepdims=True))
    return (widened * lax.rsqrt(mean_square + epsilon) * gain_vector).astype(jnp.bfloat16)

def rotate(head_values, positions):
    half_width = head_values.shape[-1] // 2
    frequency = rope_base ** (-jnp.arange(half_width, dtype=jnp.float32) / half_width)
    angles = positions.astype(jnp.float32)[:, None] * frequency[None, :]
    cosine = jnp.cos(angles)[:, None, :]
    sine_part = jnp.sin(angles)[:, None, :]
    lower_half = head_values[..., :half_width]
    upper_half = head_values[..., half_width:]
    return jnp.concatenate([lower_half * cosine - upper_half * sine_part, upper_half * cosine + lower_half * sine_part], axis=-1)

def project(row_block, gain_vector, w_qkv, positions):
    normed = rms_scale(row_block, gain_vector)
    projected = jnp.dot(normed, w_qkv, preferred_element_type=jnp.float32)
    query_width = HEADS * HEAD
    key_width = KV_HEADS * HEAD
    queries = rotate(projected[:, :query_width].reshape(-1, HEADS, HEAD), positions).astype(jnp.bfloat16)
    new_keys = rotate(projected[:, query_width:query_width + key_width].reshape(-1, KV_HEADS, HEAD), positions).astype(jnp.bfloat16)
    new_values = projected[:, query_width + key_width:].astype(jnp.bfloat16)
    return (queries, new_keys, new_values)

def request_attention(inputs):
    queries, new_keys, new_values, cache_keys, cache_values, length = inputs
    group_size = HEADS // KV_HEADS
    grouped = queries.reshape(SPAN, KV_HEADS, group_size, HEAD).astype(jnp.float32)
    all_keys = jnp.concatenate([cache_keys.reshape(CACHE, KV_HEADS, HEAD), new_keys], axis=0)
    all_values = jnp.concatenate([cache_values.reshape(CACHE, KV_HEADS, HEAD), new_values.reshape(SPAN, KV_HEADS, HEAD)], axis=0)
    query_index = jnp.arange(SPAN, dtype=jnp.int32)

    def fold_step(carried, block_index):
        best_score, running_total, running_sum = carried
        start = (block_index * KEY_BLOCK).astype(jnp.int32)
        key_part = lax.dynamic_slice_in_dim(all_keys, start, KEY_BLOCK, 0).astype(jnp.float32)
        value_part = lax.dynamic_slice_in_dim(all_values, start, KEY_BLOCK, 0).astype(jnp.float32)
        key_index = start + jnp.arange(KEY_BLOCK, dtype=jnp.int32)
        cached = (key_index < CACHE) & (key_index < length)
        in_span = (key_index >= CACHE)[None, :] & ((key_index - CACHE)[None, :] <= query_index[:, None])
        visible = (cached[None, :] | in_span)[:, None, None, :]
        scores = jnp.einsum('rkgh,bkh->rkgb', grouped, key_part) * score_scale
        block_max = lax.optimization_barrier(jnp.max(jnp.where(visible, scores, neg_big), axis=-1))
        weights = jnp.where(visible, jnp.exp(scores - block_max[..., None]), 0.0).astype(jnp.bfloat16)
        weights = lax.optimization_barrier(weights).astype(jnp.float32)
        block_total = lax.optimization_barrier(jnp.sum(weights, axis=-1))
        block_sum = jnp.einsum('rkgb,bkh->rkgh', weights, value_part)
        new_best = jnp.maximum(best_score, block_max)
        old_scale = jnp.exp(best_score - new_best)
        block_scale = jnp.exp(block_max - new_best)
        running_total = running_total * old_scale + block_total * block_scale
        running_sum = running_sum * old_scale[..., None] + block_sum * block_scale[..., None]
        return ((new_best, running_total, running_sum), None)
    initial = (jnp.full((SPAN, KV_HEADS, group_size), neg_big, jnp.float32), jnp.zeros((SPAN, KV_HEADS, group_size), jnp.float32), jnp.zeros((SPAN, KV_HEADS, group_size, HEAD), jnp.float32))
    block_count = (CACHE + SPAN) // KEY_BLOCK
    (best_score, running_total, running_sum), _ = lax.scan(fold_step, initial, jnp.arange(block_count, dtype=jnp.int32))
    return (running_sum / running_total[..., None]).astype(jnp.bfloat16).reshape(SPAN, HEADS * HEAD)

def mix_experts(expert_in, routes, route_scores, replica_slot, expert_up, expert_down):
    device_count = N_REQ * N_SEQ
    route_count = SPAN_DEV * TOP
    sentinel = TOKENS * TOP
    slot_of = jnp.take_along_axis(replica_slot, routes, axis=1).astype(jnp.int32)
    by_source = slot_of.reshape(device_count, route_count)
    onehot = (by_source[:, :, None] == jnp.arange(SLOTS, dtype=jnp.int32)[None, None, :]).astype(jnp.int32)
    slot_rank = lax.optimization_barrier(jnp.sum((jnp.cumsum(onehot, axis=1) - onehot) * onehot, axis=2)).astype(jnp.int32)
    route_ids = jnp.arange(sentinel, dtype=jnp.int32).reshape(device_count, route_count)
    device_ids = jnp.arange(device_count, dtype=jnp.int32)[:, None]
    slot_table = jnp.full((device_count, SLOTS, CAP), sentinel, jnp.int32).at[device_ids, by_source, slot_rank].set(route_ids)
    shares = (route_scores / lax.optimization_barrier(jnp.sum(route_scores, axis=1, keepdims=True))).reshape(-1)

    def slot_step(mixed_sum, slot_index):
        slot_routes = lax.dynamic_index_in_dim(slot_table, slot_index, 1, keepdims=False).reshape(-1)
        live_rows = slot_routes < sentinel
        token_index = jnp.where(live_rows, slot_routes // TOP, 0).astype(jnp.int32)
        gathered = expert_in[token_index].astype(jnp.float32) * live_rows[:, None].astype(jnp.float32)
        up_weight = lax.dynamic_index_in_dim(expert_up, slot_index, 0, keepdims=False).astype(jnp.float32)
        down_weight = lax.dynamic_index_in_dim(expert_down, slot_index, 0, keepdims=False).astype(jnp.float32)
        gate_up = jnp.dot(gathered, up_weight, precision=lax.Precision.HIGHEST)
        active = (jax.nn.silu(gate_up[:, :FF]) * gate_up[:, FF:]).astype(jnp.bfloat16)
        active = lax.optimization_barrier(active).astype(jnp.float32)
        outputs = jnp.dot(active, down_weight, precision=lax.Precision.HIGHEST).astype(jnp.bfloat16)
        outputs = lax.optimization_barrier(outputs).astype(jnp.float32)
        route_share = jnp.where(live_rows, shares[jnp.where(live_rows, slot_routes, 0)], 0.0)
        target = jnp.where(live_rows, token_index, TOKENS).astype(jnp.int32)
        mixed_sum = mixed_sum.at[target].add(outputs * route_share[:, None], mode='drop')
        return (mixed_sum, None)
    mixed_sum, _ = lax.scan(slot_step, jnp.zeros((TOKENS, D), jnp.float32), jnp.arange(SLOTS, dtype=jnp.int32))
    return mixed_sum.astype(jnp.bfloat16)

def reference(tokens, attn_gain, w_qkv, w_out, k_cache, v_cache, cache_len, ffn_gain, routes, route_scores, replica_slot, expert_up, expert_down):
    positions = (cache_len[:, None] + jnp.arange(SPAN, dtype=jnp.int32)[None, :]).reshape(-1).astype(jnp.int32)
    queries, new_keys, new_values = project(tokens, attn_gain, w_qkv, positions)
    appended = jnp.concatenate([new_keys.reshape(TOKENS, -1), new_values], axis=1)
    attended = lax.map(request_attention, (queries.reshape(REQS, SPAN, HEADS, HEAD), new_keys.reshape(REQS, SPAN, KV_HEADS, HEAD), new_values.reshape(REQS, SPAN, KV_HEADS * HEAD), k_cache, v_cache, cache_len)).reshape(TOKENS, HEADS * HEAD)
    stream = (tokens.astype(jnp.float32) + residual_scale * jnp.dot(attended, w_out, preferred_element_type=jnp.float32)).astype(jnp.bfloat16)
    expert_in = rms_scale(stream, ffn_gain)
    expert_mix = mix_experts(expert_in, routes, route_scores, replica_slot, expert_up, expert_down)
    return (attended, stream, expert_mix, appended)
```

```python
import functools
import numpy as np
import jax
import jax.numpy as jnp
from jax import lax
from jax.experimental import pallas as pl
from jax.experimental.pallas import tpu as pltpu
from jax.sharding import PartitionSpec as P

HEADS = 24
KV_HEADS = 8
HEAD = 64
CAP = 16
MESH = pl.DeviceIdType.MESH

epsilon = 1e-06
residual_scale = 0.22
score_scale = 0.015625
rope_base = 10000.0
neg_big = -1e30


def norm_rows(rows, gain):
    widened = rows.astype(jnp.float32)
    mean_square = jnp.mean(widened * widened, axis=-1, keepdims=True)
    return (widened * lax.rsqrt(mean_square + epsilon) * gain).astype(jnp.bfloat16)


def attention_kernel(
    length_ref, tokens_ref, attn_gain_ref, ffn_gain_ref, freq_ref, routes_ref, scores_ref, replica_ref,
    w_qkv_ref, w_out_ref, k_cache_ref, v_cache_ref,
    attended_ref, stream_ref, expert_in_ref, appended_ref, meta_ref,
    w_qkv, w_out, keys, values, queries, heads_out, weight_sems, cache_sems, send_sems, recv_sems,
):
    rows, width = tokens_ref.shape
    cache_half = k_cache_ref.shape[0]
    kv_width = KV_HEADS * HEAD
    q_width = HEADS * HEAD
    group = HEADS // KV_HEADS
    req, me = lax.axis_index("req"), lax.axis_index("seq")
    partner = 1 - me

    qkv_chunk = 512
    order = (3, 4, 0, 1, 2)
    weight_copies = []
    for at in order:
        cols = pl.ds(at * qkv_chunk, qkv_chunk)
        copy = pltpu.make_async_copy(w_qkv_ref.at[:, cols], w_qkv.at[:, cols], weight_sems.at[at])
        copy.start()
        weight_copies.append(copy)
    mine = pl.ds(pl.multiple_of(me * cache_half, cache_half), cache_half)
    local_k = pltpu.make_async_copy(k_cache_ref, keys.at[mine], cache_sems.at[0])
    local_v = pltpu.make_async_copy(v_cache_ref, values.at[mine], cache_sems.at[1])
    local_k.start()
    local_v.start()
    out_copy = pltpu.make_async_copy(w_out_ref, w_out, weight_sems.at[5])
    out_copy.start()

    barrier = pltpu.get_barrier_semaphore()
    pl.semaphore_signal(barrier, inc=1, device_id=(req, partner), device_id_type=MESH)
    pl.semaphore_wait(barrier, 1)

    def to_partner(src, dst, at):
        return pltpu.make_async_remote_copy(
            src_ref=src, dst_ref=dst, send_sem=send_sems.at[at], recv_sem=recv_sems.at[at],
            device_id=(req, partner), device_id_type=MESH,
        )

    send_k = to_partner(k_cache_ref, keys.at[mine], 0)
    send_v = to_partner(v_cache_ref, values.at[mine], 1)
    send_k.start()
    send_v.start()

    top = routes_ref.shape[1]
    lanes = lax.broadcasted_iota(jnp.int32, (rows, 128), 1)
    row_ids = lax.broadcasted_iota(jnp.int32, (rows, 128), 0)
    experts = replica_ref.shape[1]
    expert_lane = lax.broadcasted_iota(jnp.int32, (rows, experts), 1)
    replica = replica_ref[...].astype(jnp.float32)
    routes = routes_ref[...]
    slots = []
    hits = jnp.zeros((rows, 128), jnp.float32)
    for k in range(top):
        slot = jnp.sum(jnp.where(expert_lane == routes[:, k : k + 1], replica, 0.0), axis=1, keepdims=True)
        slots.append(slot)
        hits = hits + jnp.where(lanes == slot.astype(jnp.int32), 1.0, 0.0)
    earlier = jnp.where(row_ids > lanes, 1.0, 0.0).astype(jnp.bfloat16)
    before = jnp.dot(earlier, hits.astype(jnp.bfloat16), preferred_element_type=jnp.float32)
    scores = scores_ref[...]
    shares = scores / jnp.sum(scores, axis=1, keepdims=True)
    table = jnp.zeros((rows, 128), jnp.float32)
    for k in range(top):
        rank = jnp.sum(jnp.where(lanes == slots[k].astype(jnp.int32), before, 0.0), axis=1, keepdims=True)
        table = jnp.where(lanes == k, slots[k], table)
        table = jnp.where(lanes == top + k, rank, table)
        table = jnp.where(lanes == 2 * top + k, shares[:, k : k + 1], table)
    meta_ref[...] = jnp.transpose(table)[: meta_ref.shape[0], :].astype(meta_ref.dtype)

    normed = norm_rows(tokens_ref[...], attn_gain_ref[...])
    length = length_ref[0]
    positions = (length + me * rows + row_ids).astype(jnp.float32)
    angles = positions * freq_ref[...]
    cosine = jnp.cos(angles)
    sine = jnp.sin(angles)
    lower = (lanes % HEAD) < HEAD // 2
    signed_sine = jnp.where(lower, -sine, sine)

    def rotated(tile):
        swapped = jnp.where(lower, pltpu.roll(tile, 128 - HEAD // 2, 1), pltpu.roll(tile, HEAD // 2, 1))
        return (tile * cosine + swapped * signed_sine).astype(jnp.bfloat16)

    own_span = pl.ds(pl.multiple_of(2 * cache_half + me * rows, rows), rows)
    even_half = lanes < HEAD
    for turn, at in enumerate(order):
        weight_copies[turn].wait()
        projected = jnp.dot(
            normed, w_qkv[:, at * qkv_chunk : (at + 1) * qkv_chunk], preferred_element_type=jnp.float32
        )
        if at == 3:
            for tile in range(qkv_chunk // 128):
                new_keys = rotated(projected[:, tile * 128 : (tile + 1) * 128])
                keys[own_span, tile * 128 : (tile + 1) * 128] = new_keys
                appended_ref[:, tile * 128 : (tile + 1) * 128] = new_keys
            send_new_k = to_partner(keys.at[own_span], keys.at[own_span], 2)
            send_new_k.start()
        elif at == 4:
            new_values = projected.astype(jnp.bfloat16)
            values[own_span, :] = new_values
            appended_ref[:, kv_width:] = new_values
            send_new_v = to_partner(values.at[own_span], values.at[own_span], 3)
            send_new_v.start()
        else:
            for tile in range(qkv_chunk // 128):
                turned = rotated(projected[:, tile * 128 : (tile + 1) * 128]).astype(jnp.float32) * score_scale
                other = pltpu.roll(turned, HEAD, 1)
                for half in range(2):
                    head = (at * qkv_chunk // 128 + tile) * 2 + half
                    kv, member = head // group, head % group
                    source = turned if half == kv % 2 else other
                    keep = even_half if kv % 2 == 0 else jnp.logical_not(even_half)
                    queries[kv, member * rows : (member + 1) * rows, :] = jnp.where(keep, source, 0.0).astype(jnp.bfloat16)

    local_k.wait()
    local_v.wait()
    send_k.wait()
    send_v.wait()
    send_new_k.wait()
    send_new_v.wait()
    key_total = 2 * cache_half + 2 * rows
    key_lane = lax.broadcasted_iota(jnp.int32, (1, 2 * cache_half), 1)
    cache_bias = jnp.where(key_lane < length, 0.0, neg_big)
    span_lane = lax.broadcasted_iota(jnp.int32, (rows, 2 * rows), 1)
    span_row = lax.broadcasted_iota(jnp.int32, (rows, 2 * rows), 0) + me * rows
    span_bias = jnp.where(span_lane <= span_row, 0.0, neg_big)
    ones = jnp.ones((key_total, 128), jnp.bfloat16)
    dims = (((1,), (1,)), ((), ()))

    def one_group(kv, _):
        pair = pl.ds(pl.multiple_of((kv // 2) * 128, 128), 128)
        pair_keys = keys[:, pair]
        pair_values = jnp.concatenate([values[:, pair], ones], axis=1)
        for member in range(group):
            q = queries[kv, member * rows : (member + 1) * rows, :]
            s_cache = lax.dot_general(q, pair_keys[: 2 * cache_half], dims, preferred_element_type=jnp.float32) + cache_bias
            s_span = lax.dot_general(q, pair_keys[2 * cache_half :], dims, preferred_element_type=jnp.float32) + span_bias
            best = jnp.maximum(jnp.max(s_cache, axis=1, keepdims=True), jnp.max(s_span, axis=1, keepdims=True))
            w_cache = jnp.exp(s_cache - best).astype(jnp.bfloat16)
            w_span = jnp.exp(s_span - best).astype(jnp.bfloat16)
            summed = jnp.dot(w_cache, pair_values[: 2 * cache_half], preferred_element_type=jnp.float32)
            summed = summed + jnp.dot(w_span, pair_values[2 * cache_half :], preferred_element_type=jnp.float32)
            heads_out[kv, member * rows : (member + 1) * rows, :] = summed[:, :128] / summed[:, 128:]
        return 0

    lax.fori_loop(0, KV_HEADS, one_group, 0)

    for tile in range(q_width // 128):
        parts = []
        for half in range(2):
            head = tile * 2 + half
            kv, member = head // group, head % group
            part = heads_out[kv, member * rows : (member + 1) * rows, :]
            parts.append(part if half == kv % 2 else pltpu.roll(part, HEAD, 1))
        attended_ref[:, tile * 128 : (tile + 1) * 128] = jnp.where(even_half, parts[0], parts[1]).astype(jnp.bfloat16)

    out_copy.wait()
    attended = attended_ref[...]
    chunk = 512
    for at in range(width // chunk):
        cols = slice(at * chunk, (at + 1) * chunk)
        product = jnp.dot(attended, w_out[:, cols], preferred_element_type=jnp.float32)
        stream_ref[:, cols] = (tokens_ref[:, cols].astype(jnp.float32) + residual_scale * product).astype(jnp.bfloat16)
    expert_in_ref[...] = norm_rows(stream_ref[...], ffn_gain_ref[...])


def attention_call(tokens, attn_gain, w_qkv, w_out, k_cache, v_cache, cache_len, ffn_gain, routes, route_scores, replica_slot):
    rows, width = tokens.shape
    cache_half = k_cache.shape[1]
    kv_width = KV_HEADS * HEAD
    key_total = 2 * cache_half + 2 * rows
    half = HEAD // 2
    freq = np.float64(rope_base) ** (-(np.arange(128) % half) / half)
    freq = jnp.asarray(freq[None, :], jnp.float32)
    vmem = pl.BlockSpec(memory_space=pltpu.VMEM)
    hbm = pl.BlockSpec(memory_space=pl.ANY)
    shape = lambda *dims: jax.ShapeDtypeStruct(dims, jnp.bfloat16)
    return pl.pallas_call(
        attention_kernel,
        name="attention",
        out_shape=(shape(rows, width), shape(rows, width), shape(rows, width), shape(rows, 2 * kv_width), shape(32, 128)),
        in_specs=[pl.BlockSpec(memory_space=pltpu.SMEM)] + [vmem] * 7 + [hbm] * 4,
        out_specs=(vmem,) * 5,
        scratch_shapes=[
            pltpu.VMEM(w_qkv.shape, jnp.bfloat16),
            pltpu.VMEM(w_out.shape, jnp.bfloat16),
            pltpu.VMEM((key_total, kv_width), jnp.bfloat16),
            pltpu.VMEM((key_total, kv_width), jnp.bfloat16),
            pltpu.VMEM((KV_HEADS, HEADS // KV_HEADS * rows, 128), jnp.bfloat16),
            pltpu.VMEM((KV_HEADS, HEADS // KV_HEADS * rows, 128), jnp.float32),
            pltpu.SemaphoreType.DMA((6,)),
            pltpu.SemaphoreType.DMA((2,)),
            pltpu.SemaphoreType.DMA((4,)),
            pltpu.SemaphoreType.DMA((4,)),
        ],
        compiler_params=pltpu.CompilerParams(
            collective_id=0, has_side_effects=True, vmem_limit_bytes=60 * 1024 * 1024
        ),
    )(cache_len, tokens, attn_gain[None], ffn_gain[None], freq, routes, route_scores, replica_slot,
      w_qkv, w_out, k_cache[0], v_cache[0])


def run_experts(buffer, expert_up, expert_down):
    gate_up = jnp.einsum("sjcd,jdf->sjcf", buffer, expert_up, preferred_element_type=jnp.float32)
    hidden_width = expert_down.shape[1]
    active = (jax.nn.silu(gate_up[..., :hidden_width]) * gate_up[..., hidden_width:]).astype(
        jnp.bfloat16
    )
    return jnp.einsum(
        "sjcf,jfd->sjcd", active, expert_down, preferred_element_type=jnp.float32
    ).astype(jnp.bfloat16)


def shards(tokens, attn_gain, w_qkv, w_out, k_cache, v_cache, cache_len, ffn_gain, routes, route_scores, replica_slot, expert_up, expert_down):
    rows, width = tokens.shape
    attended, stream, expert_in, appended, meta = attention_call(
        tokens, attn_gain, w_qkv, w_out, k_cache, v_cache, cache_len, ffn_gain, routes, route_scores, replica_slot
    )
    top = routes.shape[1]
    slot_total = lax.axis_size("req") * lax.axis_size("seq")
    wide = meta.astype(jnp.float32)
    position = wide[:top] * CAP + wide[top : 2 * top]
    share = wide[2 * top : 3 * top]
    place_ids = jnp.arange(slot_total * CAP, dtype=jnp.float32)
    mix = jnp.sum(jnp.where(place_ids[None, :, None] == position[:, None, :], share[:, None, :], 0.0), axis=0)
    place = (mix > 0).astype(jnp.bfloat16)
    mix = mix.astype(jnp.bfloat16)
    outgoing = jnp.dot(place, expert_in, preferred_element_type=jnp.float32).astype(jnp.bfloat16)
    outgoing = outgoing.reshape(slot_total, 1, CAP, width)
    exchange = functools.partial(lax.all_to_all, axis_name=("req", "seq"), split_axis=0, concat_axis=0, tiled=True)
    returned = exchange(run_experts(exchange(outgoing), expert_up, expert_down)).reshape(slot_total * CAP, width)
    expert_mix = lax.dot_general(mix, returned, (((0,), (0,)), ((), ())), preferred_element_type=jnp.float32).astype(jnp.bfloat16)
    return (attended, stream, expert_mix, appended)


def solution(mesh):
    rows2 = P(("req", "seq"), None)
    rows3 = P(("req", "seq"), None, None)
    cache = P("req", "seq", None)
    return jax.shard_map(
        shards,
        mesh=mesh,
        in_specs=(rows2, P(), P(), P(), cache, cache, P("req"), P(), rows2, rows2, rows2, rows3, rows3),
        out_specs=(rows2,) * 4,
        check_vma=False,
    )
```

```python
import functools
import numpy as np
import jax
import jax.numpy as jnp
from jax import lax
from jax.experimental import pallas as pl
from jax.experimental.pallas import tpu as pltpu
from jax.sharding import PartitionSpec as P

HEADS = 24
KV_HEADS = 8
HEAD = 64
CAP = 16
MESH = pl.DeviceIdType.MESH

epsilon = 1e-06
residual_scale = 0.22
score_scale = 0.015625
rope_base = 10000.0
neg_big = -1e30


def shifted(req, dim, off):
    stride = (16, 4, 1)[dim]
    at = (req // stride) % 4
    return req + ((at + off) % 4 - at) * stride


def norm_rows(rows, gain):
    widened = rows.astype(jnp.float32)
    mean_square = jnp.mean(widened * widened, axis=-1, keepdims=True)
    return (widened * lax.rsqrt(mean_square + epsilon) * gain).astype(jnp.bfloat16)


def attention_kernel(
    length_ref, tokens_ref, attn_gain_ref, ffn_gain_ref, freq_ref, routes_ref, scores_ref, replica_ref,
    w_qkv_ref, w_out_ref, k_cache_ref, v_cache_ref,
    attended_ref, stream_ref, expert_in_ref, appended_ref, plans_ref,
    w_qkv, w_out, keys, values, queries, heads_out, plans, weight_sems, cache_sems, send_sems, recv_sems,
    plan_send, plan_recv,
):
    rows, width = tokens_ref.shape
    cache_half = k_cache_ref.shape[0]
    kv_width = KV_HEADS * HEAD
    q_width = HEADS * HEAD
    group = HEADS // KV_HEADS
    req, me = lax.axis_index("req"), lax.axis_index("seq")
    partner = 1 - me

    qkv_chunk = 512
    order = (3, 4, 0, 1, 2)
    weight_copies = []
    for at in order:
        cols = pl.ds(at * qkv_chunk, qkv_chunk)
        copy = pltpu.make_async_copy(w_qkv_ref.at[:, cols], w_qkv.at[:, cols], weight_sems.at[at])
        copy.start()
        weight_copies.append(copy)
    mine = pl.ds(pl.multiple_of(me * cache_half, cache_half), cache_half)
    local_k = pltpu.make_async_copy(k_cache_ref, keys.at[mine], cache_sems.at[0])
    local_v = pltpu.make_async_copy(v_cache_ref, values.at[mine], cache_sems.at[1])
    local_k.start()
    local_v.start()
    out_copy = pltpu.make_async_copy(w_out_ref, w_out, weight_sems.at[5])
    out_copy.start()

    barrier = pltpu.get_barrier_semaphore()
    pl.semaphore_signal(barrier, inc=1, device_id=(req, partner), device_id_type=MESH)
    for dim in range(3):
        for off in range(1, 4):
            pl.semaphore_signal(barrier, inc=1, device_id=(shifted(req, dim, off), me), device_id_type=MESH)
    pl.semaphore_wait(barrier, 10)

    def to_partner(src, dst, at):
        return pltpu.make_async_remote_copy(
            src_ref=src, dst_ref=dst, send_sem=send_sems.at[at], recv_sem=recv_sems.at[at],
            device_id=(req, partner), device_id_type=MESH,
        )

    send_k = to_partner(k_cache_ref, keys.at[mine], 0)
    send_v = to_partner(v_cache_ref, values.at[mine], 1)
    send_k.start()
    send_v.start()

    top = routes_ref.shape[0]
    lanes = lax.broadcasted_iota(jnp.int32, (rows, 128), 1)
    row_ids = lax.broadcasted_iota(jnp.int32, (rows, 128), 0)
    expert_ids = lax.broadcasted_iota(jnp.int32, replica_ref.shape, 0)
    replica = replica_ref[...]
    routes = routes_ref[...]
    slots = []
    hits = jnp.zeros((128, rows), jnp.float32)
    for k in range(top):
        slot = jnp.sum(jnp.where(expert_ids == routes[k : k + 1, :], replica, 0), axis=0, keepdims=True)
        slots.append(slot)
        hits = hits + jnp.where(row_ids == slot, 1.0, 0.0)
    earlier = jnp.where(row_ids < lanes, 1.0, 0.0).astype(jnp.bfloat16)
    before = jnp.dot(hits.astype(jnp.bfloat16), earlier, preferred_element_type=jnp.float32)
    scores = scores_ref[...]
    shares = scores / jnp.sum(scores, axis=0, keepdims=True)
    ranks = [jnp.sum(jnp.where(row_ids == slot, before, 0.0), axis=0, keepdims=True) for slot in slots]
    meta = jnp.concatenate([slot.astype(jnp.float32) for slot in slots] + ranks + [shares, shares], axis=0)
    meta = meta.astype(jnp.bfloat16)
    for f in range(3):
        plans[f, 0, 0] = meta
    plan_copies = []
    for f in range(3):
        for off in range(1, 4):
            copy = pltpu.make_async_remote_copy(
                src_ref=plans.at[f, 0, 0], dst_ref=plans.at[f, 0, 4 - off],
                send_sem=plan_send.at[f, off], recv_sem=plan_recv.at[f, off],
                device_id=(shifted(req, f, off), me), device_id_type=MESH,
            )
            copy.start()
            plan_copies.append(copy)

    normed = norm_rows(tokens_ref[...], attn_gain_ref[...])
    length = length_ref[0]
    positions = (length + me * rows + row_ids).astype(jnp.float32)
    angles = positions * freq_ref[...]
    cosine = jnp.cos(angles)
    sine = jnp.sin(angles)
    lower = (lanes % HEAD) < HEAD // 2
    signed_sine = jnp.where(lower, -sine, sine)

    def rotated(tile):
        swapped = jnp.where(lower, pltpu.roll(tile, 128 - HEAD // 2, 1), pltpu.roll(tile, HEAD // 2, 1))
        return (tile * cosine + swapped * signed_sine).astype(jnp.bfloat16)

    own_span = pl.ds(pl.multiple_of(2 * cache_half + me * rows, rows), rows)
    even_half = lanes < HEAD
    for turn, at in enumerate(order):
        weight_copies[turn].wait()
        projected = jnp.dot(
            normed, w_qkv[:, at * qkv_chunk : (at + 1) * qkv_chunk], preferred_element_type=jnp.float32
        )
        if at == 3:
            for tile in range(qkv_chunk // 128):
                new_keys = rotated(projected[:, tile * 128 : (tile + 1) * 128])
                keys[own_span, tile * 128 : (tile + 1) * 128] = new_keys
                appended_ref[:, tile * 128 : (tile + 1) * 128] = new_keys
            send_new_k = to_partner(keys.at[own_span], keys.at[own_span], 2)
            send_new_k.start()
        elif at == 4:
            new_values = projected.astype(jnp.bfloat16)
            values[own_span, :] = new_values
            appended_ref[:, kv_width:] = new_values
            send_new_v = to_partner(values.at[own_span], values.at[own_span], 3)
            send_new_v.start()
        else:
            for tile in range(qkv_chunk // 128):
                turned = rotated(projected[:, tile * 128 : (tile + 1) * 128]).astype(jnp.float32) * score_scale
                other = pltpu.roll(turned, HEAD, 1)
                for half in range(2):
                    head = (at * qkv_chunk // 128 + tile) * 2 + half
                    kv, member = head // group, head % group
                    source = turned if half == kv % 2 else other
                    keep = even_half if kv % 2 == 0 else jnp.logical_not(even_half)
                    queries[kv, member * rows : (member + 1) * rows, :] = jnp.where(keep, source, 0.0).astype(jnp.bfloat16)

    for copy in plan_copies:
        copy.wait()
    plan_copies = []
    for f in range(3):
        for off in range(1, 4):
            copy = pltpu.make_async_remote_copy(
                src_ref=plans.at[f, 0], dst_ref=plans.at[f, 4 - off],
                send_sem=plan_send.at[f, 3 + off], recv_sem=plan_recv.at[f, 3 + off],
                device_id=(shifted(req, (f + 1) % 3, off), me), device_id_type=MESH,
            )
            copy.start()
            plan_copies.append(copy)

    local_k.wait()
    local_v.wait()
    send_k.wait()
    send_v.wait()
    send_new_k.wait()
    send_new_v.wait()
    key_total = 2 * cache_half + 2 * rows
    key_lane = lax.broadcasted_iota(jnp.int32, (1, 2 * cache_half), 1)
    cache_bias = jnp.where(key_lane < length, 0.0, neg_big)
    span_lane = lax.broadcasted_iota(jnp.int32, (rows, 2 * rows), 1)
    span_row = lax.broadcasted_iota(jnp.int32, (rows, 2 * rows), 0) + me * rows
    span_bias = jnp.where(span_lane <= span_row, 0.0, neg_big)
    ones = jnp.ones((key_total, 128), jnp.bfloat16)
    dims = (((1,), (1,)), ((), ()))

    def one_group(kv, _):
        pair = pl.ds(pl.multiple_of((kv // 2) * 128, 128), 128)
        pair_keys = keys[:, pair]
        pair_values = jnp.concatenate([values[:, pair], ones], axis=1)
        for member in range(group):
            q = queries[kv, member * rows : (member + 1) * rows, :]
            s_cache = lax.dot_general(q, pair_keys[: 2 * cache_half], dims, preferred_element_type=jnp.float32) + cache_bias
            s_span = lax.dot_general(q, pair_keys[2 * cache_half :], dims, preferred_element_type=jnp.float32) + span_bias
            best = jnp.maximum(jnp.max(s_cache, axis=1, keepdims=True), jnp.max(s_span, axis=1, keepdims=True))
            w_cache = jnp.exp(s_cache - best).astype(jnp.bfloat16)
            w_span = jnp.exp(s_span - best).astype(jnp.bfloat16)
            summed = jnp.dot(w_cache, pair_values[: 2 * cache_half], preferred_element_type=jnp.float32)
            summed = summed + jnp.dot(w_span, pair_values[2 * cache_half :], preferred_element_type=jnp.float32)
            heads_out[kv, member * rows : (member + 1) * rows, :] = summed[:, :128] / summed[:, 128:]
        return 0

    lax.fori_loop(0, KV_HEADS, one_group, 0)

    for tile in range(q_width // 128):
        parts = []
        for half in range(2):
            head = tile * 2 + half
            kv, member = head // group, head % group
            part = heads_out[kv, member * rows : (member + 1) * rows, :]
            parts.append(part if half == kv % 2 else pltpu.roll(part, HEAD, 1))
        attended_ref[:, tile * 128 : (tile + 1) * 128] = jnp.where(even_half, parts[0], parts[1]).astype(jnp.bfloat16)

    out_copy.wait()
    attended = attended_ref[...]
    chunk = 512
    for at in range(width // chunk):
        cols = slice(at * chunk, (at + 1) * chunk)
        product = jnp.dot(attended, w_out[:, cols], preferred_element_type=jnp.float32)
        stream_ref[:, cols] = (tokens_ref[:, cols].astype(jnp.float32) + residual_scale * product).astype(jnp.bfloat16)
    expert_in_ref[...] = norm_rows(stream_ref[...], ffn_gain_ref[...])
    for copy in plan_copies:
        copy.wait()
    plans_ref[...] = plans[...]


def attention_call(tokens, attn_gain, w_qkv, w_out, k_cache, v_cache, cache_len, ffn_gain, routes, route_scores, replica_slot):
    rows, width = tokens.shape
    cache_half = k_cache.shape[1]
    kv_width = KV_HEADS * HEAD
    key_total = 2 * cache_half + 2 * rows
    half = HEAD // 2
    freq = np.float64(rope_base) ** (-(np.arange(128) % half) / half)
    freq = jnp.asarray(freq[None, :], jnp.float32)
    vmem = pl.BlockSpec(memory_space=pltpu.VMEM)
    hbm = pl.BlockSpec(memory_space=pl.ANY)
    shape = lambda *dims: jax.ShapeDtypeStruct(dims, jnp.bfloat16)
    return pl.pallas_call(
        attention_kernel,
        name="attention",
        out_shape=(shape(rows, width), shape(rows, width), shape(rows, width), shape(rows, 2 * kv_width), shape(3, 4, 4, 32, 128)),
        in_specs=[pl.BlockSpec(memory_space=pltpu.SMEM)] + [vmem] * 7 + [hbm] * 4,
        out_specs=(vmem,) * 5,
        scratch_shapes=[
            pltpu.VMEM(w_qkv.shape, jnp.bfloat16),
            pltpu.VMEM(w_out.shape, jnp.bfloat16),
            pltpu.VMEM((key_total, kv_width), jnp.bfloat16),
            pltpu.VMEM((key_total, kv_width), jnp.bfloat16),
            pltpu.VMEM((KV_HEADS, HEADS // KV_HEADS * rows, 128), jnp.bfloat16),
            pltpu.VMEM((KV_HEADS, HEADS // KV_HEADS * rows, 128), jnp.float32),
            pltpu.VMEM((3, 4, 4, 32, 128), jnp.bfloat16),
            pltpu.SemaphoreType.DMA((6,)),
            pltpu.SemaphoreType.DMA((2,)),
            pltpu.SemaphoreType.DMA((4,)),
            pltpu.SemaphoreType.DMA((4,)),
            pltpu.SemaphoreType.DMA((3, 7)),
            pltpu.SemaphoreType.DMA((3, 7)),
        ],
        compiler_params=pltpu.CompilerParams(
            collective_id=0, has_side_effects=True, vmem_limit_bytes=60 * 1024 * 1024
        ),
    )(cache_len, tokens, attn_gain[None], ffn_gain[None], freq, routes.T, route_scores.T, replica_slot.T,
      w_qkv, w_out, k_cache[0], v_cache[0])


def source_at(f, oa, ob):
    return (ob, oa) if f == 2 else (oa, ob)


def line_view(ref, crel, f, off):
    cols = pl.ds(f * 512, 512)
    every = slice(None)
    if f == 0:
        return ref.at[crel, every, every, off, every, cols]
    if f == 1:
        return ref.at[crel, off, every, every, every, cols]
    return ref.at[crel, every, off, every, every, cols]


def expert_kernel(
    expert_in_ref, plans_ref, up_ref, down_ref, mix_ref,
    up, down, gathered, pick, weigh, outbox, rows_in, rows_out, inbox, sums, sums_b, sums_a, send_a,
    weight_sems, local_sems, send1, recv1, send2, recv2, send3, recv3, send4, recv4, send5, recv5, send6, recv6,
):
    tokens = expert_in_ref.shape[0]
    req, me = lax.axis_index("req"), lax.axis_index("seq")
    up_copy = pltpu.make_async_copy(up_ref, up, weight_sems.at[0])
    down_copy = pltpu.make_async_copy(down_ref, down, weight_sems.at[1])
    up_copy.start()
    down_copy.start()

    barrier = pltpu.get_barrier_semaphore()
    pl.semaphore_signal(barrier, inc=1, device_id=(req, 1 - me), device_id_type=MESH)
    for dim in range(3):
        for off in range(1, 4):
            for core in range(2):
                pl.semaphore_signal(barrier, inc=1, device_id=(shifted(req, dim, off), core), device_id_type=MESH)
    pl.semaphore_wait(barrier, 19)

    def send(src, dst, send_sem, recv_sem, dim, off, crel=0):
        core = me if crel == 0 else 1 - me
        copy = pltpu.make_async_remote_copy(
            src_ref=src, dst_ref=dst, send_sem=send_sem, recv_sem=recv_sem,
            device_id=(shifted(req, dim, off), core), device_id_type=MESH,
        )
        copy.start()
        return copy

    half = tokens // 2
    low, high = pl.ds(0, half), pl.ds(half, half)

    def block(f, ob, oa):
        if ob == 0 and oa == 0:
            return expert_in_ref.at[:, pl.ds(f * 512, 512)]
        return gathered.at[f, ob, oa]

    first, second = {}, {}

    def start_second(f, oa):
        b = (f + 1) % 3
        second[f, oa, 0] = send(block(f, 0, oa), gathered.at[f, 3, oa], send2.at[f, oa, 0], recv2.at[f, oa, 0], b, 1)
        second[f, oa, 1] = send(block(f, 0, oa), gathered.at[f, 1, oa], send2.at[f, oa, 1], recv2.at[f, oa, 1], b, 3)

    def forward_second(f, oa):
        b = (f + 1) % 3
        second[f, oa, 0].wait_recv()
        second[f, oa, 2] = send(
            gathered.at[f, 3, oa, low], gathered.at[f, 2, oa, low], send2.at[f, oa, 2], recv2.at[f, oa, 2], b, 1)
        second[f, oa, 1].wait_recv()
        second[f, oa, 3] = send(
            gathered.at[f, 1, oa, high], gathered.at[f, 2, oa, high], send2.at[f, oa, 3], recv2.at[f, oa, 3], b, 3)

    for f in range(3):
        first[f, 0] = send(block(f, 0, 0), gathered.at[f, 0, 3], send1.at[f, 0], recv1.at[f, 0], f, 1)
        first[f, 1] = send(block(f, 0, 0), gathered.at[f, 0, 1], send1.at[f, 1], recv1.at[f, 1], f, 3)
    for f in range(3):
        start_second(f, 0)

    line_row = lax.broadcasted_iota(jnp.int32, (128, 128), 0)
    row_crel, row_off, row_rank = line_row // 64, (line_row // 16) % 4, line_row % 16

    def build(f):
        stride = (16, 4, 1)[(f + 2) % 3]
        at = (req // stride) % 4
        target_req = req + ((at + row_off) % 4 - at) * stride
        target_core = me + row_crel - 2 * me * row_crel
        target = ((2 * target_req + target_core) * CAP + row_rank).astype(jnp.float32)
        for ob in range(4):
            def one(oa, _):
                plan = plans_ref[f, ob, oa].astype(jnp.float32)
                position = plan[:8] * CAP + plan[8:16]
                chosen = jnp.zeros((128, 128), jnp.float32)
                for k in range(8):
                    chosen = jnp.where(target == position[k : k + 1, :], plan[16 + k : 17 + k, :], chosen)
                pick[f, ob, oa] = jnp.where(chosen > 0.0, 1.0, 0.0).astype(jnp.bfloat16)
                weigh[f, ob, oa] = jnp.transpose(chosen).astype(jnp.bfloat16)
                return 0
            lax.fori_loop(0, 4, one, 0)

    def select(f, ob, oa):
        d1, d2 = source_at(f, oa, ob)
        rows = jnp.dot(pick[f, ob, oa], block(f, ob, oa)[...], preferred_element_type=jnp.float32)
        outbox[f, :, :, d1, d2] = rows.astype(jnp.bfloat16).reshape(2, 4, CAP, 512)

    build(0)
    for f in range(3):
        first[f, 0].wait_recv()
        first[f, 2] = send(
            gathered.at[f, 0, 3, low], gathered.at[f, 0, 2, low], send1.at[f, 2], recv1.at[f, 2], f, 1)
        first[f, 1].wait_recv()
        first[f, 3] = send(
            gathered.at[f, 0, 1, high], gathered.at[f, 0, 2, high], send1.at[f, 3], recv1.at[f, 3], f, 3)
    for f in range(3):
        forward_second(f, 0)
        start_second(f, 3)
        start_second(f, 1)
    build(1)
    for f in range(3):
        first[f, 2].wait_recv()
        first[f, 3].wait_recv()
        start_second(f, 2)
    build(2)
    for f in range(3):
        for oa in range(4):
            select(f, 0, oa)
        for ob in (1, 3):
            select(f, ob, 0)
    for oa in (3, 1, 2):
        for f in range(3):
            forward_second(f, oa)
        for f in range(3):
            for ob in (1, 3):
                select(f, ob, oa)
    for oa in (0, 3, 1, 2):
        for f in range(3):
            second[f, oa, 2].wait_recv()
            second[f, oa, 3].wait_recv()
            select(f, 2, oa)

    out, back = {}, {}
    for crel in range(2):
        for off in (2, 1, 3, 0):
            for f in range(3):
                src, dst = outbox.at[f, crel, off], line_view(rows_in, crel, f, (4 - off) % 4)
                if crel == 0 and off == 0:
                    copy = pltpu.make_async_copy(src, dst, local_sems.at[f])
                    copy.start()
                else:
                    copy = send(src, dst, send3.at[f, crel, off], recv3.at[f, crel, off], (f + 2) % 3, off, crel)
                out[f, crel, off] = copy

    up_copy.wait()
    down_copy.wait()
    hidden = down.shape[0]
    for crel in range(2):
        for off in range(4):
            for f in range(3):
                if crel == 0 and off == 0:
                    out[f, crel, off].wait()
                else:
                    out[f, crel, off].wait_recv()

        def experts(oz, _):
            rows = rows_in[crel, oz].reshape(256, rows_in.shape[-1])
            gate = jnp.dot(rows, up[:, :hidden], preferred_element_type=jnp.float32)
            lift = jnp.dot(rows, up[:, hidden:], preferred_element_type=jnp.float32)
            active = (gate / (1.0 + jnp.exp(-gate)) * lift).astype(jnp.bfloat16)
            result = jnp.dot(active, down[...], preferred_element_type=jnp.float32)
            rows_out[crel, oz] = result.astype(jnp.bfloat16).reshape(rows_out.shape[2:])
            return 0

        lax.fori_loop(0, 4, experts, 0)
        for off in (2, 1, 3, 0):
            for f in range(3):
                src, dst = line_view(rows_out, crel, f, off), inbox.at[f, crel, (4 - off) % 4]
                if crel == 0 and off == 0:
                    copy = pltpu.make_async_copy(src, dst, local_sems.at[3 + f])
                    copy.start()
                else:
                    copy = send(src, dst, send4.at[f, crel, off], recv4.at[f, crel, off], (f + 2) % 3, off, crel)
                back[f, crel, off] = copy

    for key, copy in back.items():
        if key[1:] == (0, 0):
            copy.wait()
        else:
            copy.wait_recv()

    def line_sum(f, ob, oa):
        d1, d2 = source_at(f, oa, ob)
        rows = inbox[f, :, :, d1, d2].reshape(128, 512)
        return jnp.dot(weigh[f, ob, oa], rows, preferred_element_type=jnp.float32)

    along_b, along_a = {}, {}
    for oa in (2, 1, 3, 0):
        for ob in (2, 1, 3):
            for f in range(3):
                sums[f, ob, oa] = line_sum(f, ob, oa).astype(jnp.bfloat16)
                along_b[f, ob, oa] = send(
                    sums.at[f, ob, oa], sums_b.at[f, ob - 1, oa],
                    send5.at[f, ob, oa], recv5.at[f, ob, oa], (f + 1) % 3, ob)
    for f in range(3):
        for oa in range(4):
            sums[f, 0, oa] = line_sum(f, 0, oa).astype(jnp.bfloat16)
    own = {}
    for oa in (2, 1, 3, 0):
        for f in range(3):
            total = sums[f, 0, oa].astype(jnp.float32)
            for ob in (2, 1, 3):
                along_b[f, ob, oa].wait_recv()
                total = total + sums_b[f, ob - 1, oa].astype(jnp.float32)
            if oa == 0:
                own[f] = total
            else:
                send_a[f, oa - 1] = total.astype(jnp.bfloat16)
                along_a[f, oa] = send(
                    send_a.at[f, oa - 1], sums_a.at[f, oa - 1], send6.at[f, oa], recv6.at[f, oa], f, oa)
    for f in range(3):
        total = own[f]
        for oa in (2, 1, 3):
            along_a[f, oa].wait_recv()
            total = total + sums_a[f, oa - 1].astype(jnp.float32)
        mix_ref[:, f * 512 : (f + 1) * 512] = total.astype(jnp.bfloat16)

    for name, copies in enumerate((first, second, along_b, along_a, out, back)):
        for key, copy in copies.items():
            if name < 4 or key[1:] != (0, 0):
                copy.wait_send()


def expert_call(expert_in, plans, expert_up, expert_down):
    tokens, width = expert_in.shape
    vmem = pl.BlockSpec(memory_space=pltpu.VMEM)
    hbm = pl.BlockSpec(memory_space=pl.ANY)
    half = lambda *dims: pltpu.VMEM(dims, jnp.bfloat16)
    sems = lambda *dims: pltpu.SemaphoreType.DMA(dims)
    pairs = lambda *dims: [sems(*dims), sems(*dims)]
    return pl.pallas_call(
        expert_kernel,
        name="experts",
        out_shape=jax.ShapeDtypeStruct((tokens, width), jnp.bfloat16),
        in_specs=[vmem, vmem, hbm, hbm],
        out_specs=vmem,
        scratch_shapes=[
            half(*expert_up.shape[1:]),
            half(*expert_down.shape[1:]),
            half(3, 4, 4, tokens, 512),
            half(3, 4, 4, 128, 128),
            half(3, 4, 4, 128, 128),
            half(3, 2, 4, 4, 4, CAP, 512),
            half(2, 4, 4, 4, CAP, width),
            half(2, 4, 4, 4, CAP, width),
            half(3, 2, 4, 4, 4, CAP, 512),
            half(3, 4, 4, tokens, 512),
            half(3, 3, 4, tokens, 512),
            half(3, 3, tokens, 512),
            half(3, 3, tokens, 512),
            sems(2), sems(6),
        ]
        + pairs(3, 4) + pairs(3, 4, 4) + pairs(3, 2, 4) + pairs(3, 2, 4) + pairs(3, 4, 4) + pairs(3, 4),
        compiler_params=pltpu.CompilerParams(
            collective_id=1, has_side_effects=True, vmem_limit_bytes=67043328
        ),
    )(expert_in, plans, expert_up[0], expert_down[0])


def shards(tokens, attn_gain, w_qkv, w_out, k_cache, v_cache, cache_len, ffn_gain, routes, route_scores, replica_slot, expert_up, expert_down):
    attended, stream, expert_in, appended, plans = attention_call(
        tokens, attn_gain, w_qkv, w_out, k_cache, v_cache, cache_len, ffn_gain, routes, route_scores, replica_slot
    )
    expert_mix = expert_call(expert_in, plans, expert_up, expert_down)
    return (attended, stream, expert_mix, appended)


def solution(mesh):
    rows2 = P(("req", "seq"), None)
    rows3 = P(("req", "seq"), None, None)
    cache = P("req", "seq", None)
    return jax.shard_map(
        shards,
        mesh=mesh,
        in_specs=(rows2, P(), P(), P(), cache, cache, P("req"), P(), rows2, rows2, rows2, rows3, rows3),
        out_specs=(rows2,) * 4,
        check_vma=False,
    )
```

```python
import functools
import numpy as np
import jax
import jax.numpy as jnp
from jax import lax
from jax.experimental import pallas as pl
from jax.experimental.pallas import tpu as pltpu
from jax.sharding import PartitionSpec as P

HEADS = 24
KV_HEADS = 8
HEAD = 64
CAP = 16
MESH = pl.DeviceIdType.MESH

epsilon = 1e-06
residual_scale = 0.22
score_scale = 0.015625
rope_base = 10000.0
neg_big = -1e30


def shifted(req, dim, off):
    stride = (16, 4, 1)[dim]
    at = (req // stride) % 4
    return req + ((at + off) % 4 - at) * stride


def norm_rows(rows, gain):
    widened = rows.astype(jnp.float32)
    mean_square = jnp.mean(widened * widened, axis=-1, keepdims=True)
    return (widened * lax.rsqrt(mean_square + epsilon) * gain).astype(jnp.bfloat16)


def attention_kernel(
    length_ref, tokens_ref, attn_gain_ref, ffn_gain_ref, freq_ref, routes_ref, scores_ref, replica_ref,
    w_qkv_ref, w_out_ref, k_cache_ref, v_cache_ref,
    attended_ref, stream_ref, expert_in_ref, appended_ref, plans_ref,
    w_qkv, w_out, keys, values, queries, heads_out, plans, weight_sems, cache_sems, send_sems, recv_sems,
    plan_send, plan_recv,
):
    rows, width = tokens_ref.shape
    cache_half = k_cache_ref.shape[0]
    kv_width = KV_HEADS * HEAD
    q_width = HEADS * HEAD
    group = HEADS // KV_HEADS
    req, me = lax.axis_index("req"), lax.axis_index("seq")
    partner = 1 - me

    qkv_chunk = 512
    order = (3, 4, 0, 1, 2)
    weight_copies = []
    for at in order:
        cols = pl.ds(at * qkv_chunk, qkv_chunk)
        copy = pltpu.make_async_copy(w_qkv_ref.at[:, cols], w_qkv.at[:, cols], weight_sems.at[at])
        copy.start()
        weight_copies.append(copy)
    mine = pl.ds(pl.multiple_of(me * cache_half, cache_half), cache_half)
    local_k = pltpu.make_async_copy(k_cache_ref, keys.at[mine], cache_sems.at[0])
    local_v = pltpu.make_async_copy(v_cache_ref, values.at[mine], cache_sems.at[1])
    local_k.start()
    local_v.start()
    out_copy = pltpu.make_async_copy(w_out_ref, w_out, weight_sems.at[5])
    out_copy.start()

    barrier = pltpu.get_barrier_semaphore()
    pl.semaphore_signal(barrier, inc=1, device_id=(req, partner), device_id_type=MESH)
    for dim in range(3):
        for off in range(1, 4):
            pl.semaphore_signal(barrier, inc=1, device_id=(shifted(req, dim, off), me), device_id_type=MESH)
    pl.semaphore_wait(barrier, 10)

    def to_partner(src, dst, at):
        return pltpu.make_async_remote_copy(
            src_ref=src, dst_ref=dst, send_sem=send_sems.at[at], recv_sem=recv_sems.at[at],
            device_id=(req, partner), device_id_type=MESH,
        )

    send_k = to_partner(k_cache_ref, keys.at[mine], 0)
    send_v = to_partner(v_cache_ref, values.at[mine], 1)
    send_k.start()
    send_v.start()

    top = routes_ref.shape[0]
    lanes = lax.broadcasted_iota(jnp.int32, (rows, 128), 1)
    row_ids = lax.broadcasted_iota(jnp.int32, (rows, 128), 0)
    expert_ids = lax.broadcasted_iota(jnp.int32, replica_ref.shape, 0)
    replica = replica_ref[...]
    routes = routes_ref[...]
    slots = []
    hits = jnp.zeros((128, rows), jnp.float32)
    for k in range(top):
        slot = jnp.sum(jnp.where(expert_ids == routes[k : k + 1, :], replica, 0), axis=0, keepdims=True)
        slots.append(slot)
        hits = hits + jnp.where(row_ids == slot, 1.0, 0.0)
    earlier = jnp.where(row_ids < lanes, 1.0, 0.0).astype(jnp.bfloat16)
    before = jnp.dot(hits.astype(jnp.bfloat16), earlier, preferred_element_type=jnp.float32)
    scores = scores_ref[...]
    shares = scores / jnp.sum(scores, axis=0, keepdims=True)
    ranks = [jnp.sum(jnp.where(row_ids == slot, before, 0.0), axis=0, keepdims=True) for slot in slots]
    meta = jnp.concatenate([slot.astype(jnp.float32) for slot in slots] + ranks + [shares, shares], axis=0)
    meta = meta.astype(jnp.bfloat16)
    for f in range(3):
        plans[f, 0, 0] = meta
    plan_copies = []
    for f in range(3):
        for off in range(1, 4):
            copy = pltpu.make_async_remote_copy(
                src_ref=plans.at[f, 0, 0], dst_ref=plans.at[f, 0, 4 - off],
                send_sem=plan_send.at[f, off], recv_sem=plan_recv.at[f, off],
                device_id=(shifted(req, f, off), me), device_id_type=MESH,
            )
            copy.start()
            plan_copies.append(copy)

    normed = norm_rows(tokens_ref[...], attn_gain_ref[...].reshape(1, width))
    length = length_ref[0]
    positions = (length + me * rows + row_ids).astype(jnp.float32)
    angles = positions * freq_ref[...]
    cosine = jnp.cos(angles)
    sine = jnp.sin(angles)
    lower = (lanes % HEAD) < HEAD // 2
    signed_sine = jnp.where(lower, -sine, sine)

    def rotated(tile):
        swapped = jnp.where(lower, pltpu.roll(tile, 128 - HEAD // 2, 1), pltpu.roll(tile, HEAD // 2, 1))
        return (tile * cosine + swapped * signed_sine).astype(jnp.bfloat16)

    own_span = pl.ds(pl.multiple_of(2 * cache_half + me * rows, rows), rows)
    even_half = lanes < HEAD
    for turn, at in enumerate(order):
        weight_copies[turn].wait()
        projected = jnp.dot(
            normed, w_qkv[:, at * qkv_chunk : (at + 1) * qkv_chunk], preferred_element_type=jnp.float32
        )
        if at == 3:
            for tile in range(qkv_chunk // 128):
                new_keys = rotated(projected[:, tile * 128 : (tile + 1) * 128])
                keys[own_span, tile * 128 : (tile + 1) * 128] = new_keys
                appended_ref[:, tile * 128 : (tile + 1) * 128] = new_keys
            send_new_k = to_partner(keys.at[own_span], keys.at[own_span], 2)
            send_new_k.start()
        elif at == 4:
            new_values = projected.astype(jnp.bfloat16)
            values[own_span, :] = new_values
            appended_ref[:, kv_width:] = new_values
            send_new_v = to_partner(values.at[own_span], values.at[own_span], 3)
            send_new_v.start()
        else:
            for tile in range(qkv_chunk // 128):
                turned = rotated(projected[:, tile * 128 : (tile + 1) * 128]).astype(jnp.float32) * score_scale
                other = pltpu.roll(turned, HEAD, 1)
                for half in range(2):
                    head = (at * qkv_chunk // 128 + tile) * 2 + half
                    kv, member = head // group, head % group
                    source = turned if half == kv % 2 else other
                    keep = even_half if kv % 2 == 0 else jnp.logical_not(even_half)
                    queries[kv, member * rows : (member + 1) * rows, :] = jnp.where(keep, source, 0.0).astype(jnp.bfloat16)

    for copy in plan_copies:
        copy.wait()
    plan_copies = []
    for f in range(3):
        for off in range(1, 4):
            copy = pltpu.make_async_remote_copy(
                src_ref=plans.at[f, 0], dst_ref=plans.at[f, 4 - off],
                send_sem=plan_send.at[f, 3 + off], recv_sem=plan_recv.at[f, 3 + off],
                device_id=(shifted(req, (f + 1) % 3, off), me), device_id_type=MESH,
            )
            copy.start()
            plan_copies.append(copy)

    local_k.wait()
    local_v.wait()
    send_k.wait()
    send_v.wait()
    send_new_k.wait()
    send_new_v.wait()
    key_total = 2 * cache_half + 2 * rows
    key_lane = lax.broadcasted_iota(jnp.int32, (1, 2 * cache_half), 1)
    cache_bias = jnp.where(key_lane < length, 0.0, neg_big)
    span_lane = lax.broadcasted_iota(jnp.int32, (rows, 2 * rows), 1)
    span_row = lax.broadcasted_iota(jnp.int32, (rows, 2 * rows), 0) + me * rows
    span_bias = jnp.where(span_lane <= span_row, 0.0, neg_big)
    ones = jnp.ones((key_total, 128), jnp.bfloat16)
    dims = (((1,), (1,)), ((), ()))

    def one_group(kv, _):
        pair = pl.ds(pl.multiple_of((kv // 2) * 128, 128), 128)
        pair_keys = keys[:, pair]
        pair_values = jnp.concatenate([values[:, pair], ones], axis=1)
        for member in range(group):
            q = queries[kv, member * rows : (member + 1) * rows, :]
            s_cache = lax.dot_general(q, pair_keys[: 2 * cache_half], dims, preferred_element_type=jnp.float32) + cache_bias
            s_span = lax.dot_general(q, pair_keys[2 * cache_half :], dims, preferred_element_type=jnp.float32) + span_bias
            best = jnp.maximum(jnp.max(s_cache, axis=1, keepdims=True), jnp.max(s_span, axis=1, keepdims=True))
            w_cache = jnp.exp(s_cache - best).astype(jnp.bfloat16)
            w_span = jnp.exp(s_span - best).astype(jnp.bfloat16)
            summed = jnp.dot(w_cache, pair_values[: 2 * cache_half], preferred_element_type=jnp.float32)
            summed = summed + jnp.dot(w_span, pair_values[2 * cache_half :], preferred_element_type=jnp.float32)
            heads_out[kv, member * rows : (member + 1) * rows, :] = summed[:, :128] / summed[:, 128:]
        return 0

    lax.fori_loop(0, KV_HEADS, one_group, 0)

    for tile in range(q_width // 128):
        parts = []
        for half in range(2):
            head = tile * 2 + half
            kv, member = head // group, head % group
            part = heads_out[kv, member * rows : (member + 1) * rows, :]
            parts.append(part if half == kv % 2 else pltpu.roll(part, HEAD, 1))
        attended_ref[:, tile * 128 : (tile + 1) * 128] = jnp.where(even_half, parts[0], parts[1]).astype(jnp.bfloat16)

    out_copy.wait()
    attended = attended_ref[...]
    chunk = 512
    for at in range(width // chunk):
        cols = slice(at * chunk, (at + 1) * chunk)
        product = jnp.dot(attended, w_out[:, cols], preferred_element_type=jnp.float32)
        stream_ref[:, cols] = (tokens_ref[:, cols].astype(jnp.float32) + residual_scale * product).astype(jnp.bfloat16)
    expert_in_ref[...] = norm_rows(stream_ref[...], ffn_gain_ref[...].reshape(1, width))
    for copy in plan_copies:
        copy.wait()
    plans_ref[...] = plans[...]


def attention_call(tokens, attn_gain, w_qkv, w_out, k_cache, v_cache, cache_len, ffn_gain, routes, route_scores, replica_slot):
    rows, width = tokens.shape
    cache_half = k_cache.shape[1]
    kv_width = KV_HEADS * HEAD
    key_total = 2 * cache_half + 2 * rows
    half = HEAD // 2
    freq = np.float64(rope_base) ** (-(np.arange(128) % half) / half)
    freq = jnp.asarray(freq[None, :], jnp.float32)
    vmem = pl.BlockSpec(memory_space=pltpu.VMEM)
    hbm = pl.BlockSpec(memory_space=pl.ANY)
    shape = lambda *dims: jax.ShapeDtypeStruct(dims, jnp.bfloat16)
    return pl.pallas_call(
        attention_kernel,
        name="attention",
        out_shape=(shape(rows, width), shape(rows, width), shape(rows, width), shape(rows, 2 * kv_width), shape(3, 4, 4, 32, 128)),
        in_specs=[pl.BlockSpec(memory_space=pltpu.SMEM)] + [vmem] * 7 + [hbm] * 4,
        out_specs=(vmem,) * 5,
        scratch_shapes=[
            pltpu.VMEM(w_qkv.shape, jnp.bfloat16),
            pltpu.VMEM(w_out.shape, jnp.bfloat16),
            pltpu.VMEM((key_total, kv_width), jnp.bfloat16),
            pltpu.VMEM((key_total, kv_width), jnp.bfloat16),
            pltpu.VMEM((KV_HEADS, HEADS // KV_HEADS * rows, 128), jnp.bfloat16),
            pltpu.VMEM((KV_HEADS, HEADS // KV_HEADS * rows, 128), jnp.float32),
            pltpu.VMEM((3, 4, 4, 32, 128), jnp.bfloat16),
            pltpu.SemaphoreType.DMA((6,)),
            pltpu.SemaphoreType.DMA((2,)),
            pltpu.SemaphoreType.DMA((4,)),
            pltpu.SemaphoreType.DMA((4,)),
            pltpu.SemaphoreType.DMA((3, 7)),
            pltpu.SemaphoreType.DMA((3, 7)),
        ],
        compiler_params=pltpu.CompilerParams(
            collective_id=0, has_side_effects=True, vmem_limit_bytes=60 * 1024 * 1024
        ),
    )(cache_len, tokens, attn_gain, ffn_gain, freq, routes.T, route_scores.T, replica_slot.T,
      w_qkv, w_out, k_cache[0], v_cache[0])


def source_at(f, oa, ob):
    return (ob, oa) if f == 2 else (oa, ob)


def line_view(ref, crel, f, off):
    cols = pl.ds(f * 512, 512)
    every = slice(None)
    if f == 0:
        return ref.at[crel, every, every, off, every, cols]
    if f == 1:
        return ref.at[crel, off, every, every, every, cols]
    return ref.at[crel, every, off, every, every, cols]


def expert_kernel(
    expert_in_ref, plans_ref, up_ref, down_ref, mix_ref,
    up, down, gathered, pick, weigh, outbox, rows_in, rows_out, inbox, sums, sums_b, sums_a, send_a,
    weight_sems, local_sems, send1, recv1, send2, recv2, send3, recv3, send4, recv4, send5, recv5, send6, recv6,
):
    tokens = expert_in_ref.shape[0]
    req, me = lax.axis_index("req"), lax.axis_index("seq")
    up_copy = pltpu.make_async_copy(up_ref, up, weight_sems.at[0])
    down_copy = pltpu.make_async_copy(down_ref, down, weight_sems.at[1])
    up_copy.start()
    down_copy.start()

    barrier = pltpu.get_barrier_semaphore()
    pl.semaphore_signal(barrier, inc=1, device_id=(req, 1 - me), device_id_type=MESH)
    for dim in range(3):
        for off in range(1, 4):
            for core in range(2):
                pl.semaphore_signal(barrier, inc=1, device_id=(shifted(req, dim, off), core), device_id_type=MESH)
    pl.semaphore_wait(barrier, 19)

    def send(src, dst, send_sem, recv_sem, dim, off, crel=0):
        core = me if crel == 0 else 1 - me
        copy = pltpu.make_async_remote_copy(
            src_ref=src, dst_ref=dst, send_sem=send_sem, recv_sem=recv_sem,
            device_id=(shifted(req, dim, off), core), device_id_type=MESH,
        )
        copy.start()
        return copy

    half = tokens // 2
    low, high = pl.ds(0, half), pl.ds(half, half)

    def block(f, ob, oa):
        if ob == 0 and oa == 0:
            return expert_in_ref.at[:, pl.ds(f * 512, 512)]
        return gathered.at[f, ob, oa]

    first, second = {}, {}

    def start_second(f, oa):
        b = (f + 1) % 3
        second[f, oa, 0] = send(block(f, 0, oa), gathered.at[f, 3, oa], send2.at[f, oa, 0], recv2.at[f, oa, 0], b, 1)
        second[f, oa, 1] = send(block(f, 0, oa), gathered.at[f, 1, oa], send2.at[f, oa, 1], recv2.at[f, oa, 1], b, 3)

    def forward_second(f, oa):
        b = (f + 1) % 3
        second[f, oa, 0].wait_recv()
        second[f, oa, 2] = send(
            gathered.at[f, 3, oa, low], gathered.at[f, 2, oa, low], send2.at[f, oa, 2], recv2.at[f, oa, 2], b, 1)
        second[f, oa, 1].wait_recv()
        second[f, oa, 3] = send(
            gathered.at[f, 1, oa, high], gathered.at[f, 2, oa, high], send2.at[f, oa, 3], recv2.at[f, oa, 3], b, 3)

    for f in range(3):
        first[f, 0] = send(block(f, 0, 0), gathered.at[f, 0, 3], send1.at[f, 0], recv1.at[f, 0], f, 1)
        first[f, 1] = send(block(f, 0, 0), gathered.at[f, 0, 1], send1.at[f, 1], recv1.at[f, 1], f, 3)
    for f in range(3):
        start_second(f, 0)

    line_row = lax.broadcasted_iota(jnp.int32, (128, 128), 0)
    row_crel, row_off, row_rank = line_row // 64, (line_row // 16) % 4, line_row % 16

    def build(f):
        stride = (16, 4, 1)[(f + 2) % 3]
        at = (req // stride) % 4
        target_req = req + ((at + row_off) % 4 - at) * stride
        target_core = me + row_crel - 2 * me * row_crel
        target = ((2 * target_req + target_core) * CAP + row_rank).astype(jnp.float32)
        for ob in range(4):
            def one(oa, _):
                plan = plans_ref[f, ob, oa].astype(jnp.float32)
                position = plan[:8] * CAP + plan[8:16]
                chosen = jnp.zeros((128, 128), jnp.float32)
                for k in range(8):
                    chosen = jnp.where(target == position[k : k + 1, :], plan[16 + k : 17 + k, :], chosen)
                pick[f, ob, oa] = jnp.where(chosen > 0.0, 1.0, 0.0).astype(jnp.bfloat16)
                weigh[f, ob, oa] = jnp.transpose(chosen).astype(jnp.bfloat16)
                return 0
            lax.fori_loop(0, 4, one, 0)

    def select(f, ob, oa):
        d1, d2 = source_at(f, oa, ob)
        rows = jnp.dot(pick[f, ob, oa], block(f, ob, oa)[...], preferred_element_type=jnp.float32)
        outbox[f, :, :, d1, d2] = rows.astype(jnp.bfloat16).reshape(2, 4, CAP, 512)

    build(0)
    for f in range(3):
        first[f, 0].wait_recv()
        first[f, 2] = send(
            gathered.at[f, 0, 3, low], gathered.at[f, 0, 2, low], send1.at[f, 2], recv1.at[f, 2], f, 1)
        first[f, 1].wait_recv()
        first[f, 3] = send(
            gathered.at[f, 0, 1, high], gathered.at[f, 0, 2, high], send1.at[f, 3], recv1.at[f, 3], f, 3)
    for f in range(3):
        forward_second(f, 0)
        start_second(f, 3)
        start_second(f, 1)
    build(1)
    for f in range(3):
        first[f, 2].wait_recv()
        first[f, 3].wait_recv()
        start_second(f, 2)
    build(2)
    for f in range(3):
        for oa in range(4):
            select(f, 0, oa)
        for ob in (1, 3):
            select(f, ob, 0)
    for oa in (3, 1, 2):
        for f in range(3):
            forward_second(f, oa)
        for f in range(3):
            for ob in (1, 3):
                select(f, ob, oa)
    for oa in (0, 3, 1, 2):
        for f in range(3):
            second[f, oa, 2].wait_recv()
            second[f, oa, 3].wait_recv()
            select(f, 2, oa)

    out, back = {}, {}
    for crel in range(2):
        for off in (2, 1, 3, 0):
            for f in range(3):
                src, dst = outbox.at[f, crel, off], line_view(rows_in, crel, f, (4 - off) % 4)
                if crel == 0 and off == 0:
                    copy = pltpu.make_async_copy(src, dst, local_sems.at[f])
                    copy.start()
                else:
                    copy = send(src, dst, send3.at[f, crel, off], recv3.at[f, crel, off], (f + 2) % 3, off, crel)
                out[f, crel, off] = copy

    up_copy.wait()
    down_copy.wait()
    hidden = down.shape[0]
    for crel in range(2):
        for off in range(4):
            for f in range(3):
                if crel == 0 and off == 0:
                    out[f, crel, off].wait()
                else:
                    out[f, crel, off].wait_recv()

        def experts(oz, _):
            rows = rows_in[crel, oz].reshape(256, rows_in.shape[-1])
            gate = jnp.dot(rows, up[:, :hidden], preferred_element_type=jnp.float32)
            lift = jnp.dot(rows, up[:, hidden:], preferred_element_type=jnp.float32)
            active = (gate / (1.0 + jnp.exp(-gate)) * lift).astype(jnp.bfloat16)
            result = jnp.dot(active, down[...], preferred_element_type=jnp.float32)
            rows_out[crel, oz] = result.astype(jnp.bfloat16).reshape(rows_out.shape[2:])
            return 0

        lax.fori_loop(0, 4, experts, 0)
        for off in (2, 1, 3, 0):
            for f in range(3):
                src, dst = line_view(rows_out, crel, f, off), inbox.at[f, crel, (4 - off) % 4]
                if crel == 0 and off == 0:
                    copy = pltpu.make_async_copy(src, dst, local_sems.at[3 + f])
                    copy.start()
                else:
                    copy = send(src, dst, send4.at[f, crel, off], recv4.at[f, crel, off], (f + 2) % 3, off, crel)
                back[f, crel, off] = copy

    for key, copy in back.items():
        if key[1:] == (0, 0):
            copy.wait()
        else:
            copy.wait_recv()

    def line_sum(f, ob, oa):
        d1, d2 = source_at(f, oa, ob)
        rows = inbox[f, :, :, d1, d2].reshape(128, 512)
        return jnp.dot(weigh[f, ob, oa], rows, preferred_element_type=jnp.float32)

    along_b, along_a = {}, {}
    for oa in (2, 1, 3, 0):
        for ob in (2, 1, 3):
            for f in range(3):
                sums[f, ob, oa] = line_sum(f, ob, oa).astype(jnp.bfloat16)
                along_b[f, ob, oa] = send(
                    sums.at[f, ob, oa], sums_b.at[f, ob - 1, oa],
                    send5.at[f, ob, oa], recv5.at[f, ob, oa], (f + 1) % 3, ob)
    for f in range(3):
        for oa in range(4):
            sums[f, 0, oa] = line_sum(f, 0, oa).astype(jnp.bfloat16)
    own = {}
    for oa in (2, 1, 3, 0):
        for f in range(3):
            total = sums[f, 0, oa].astype(jnp.float32)
            for ob in (2, 1, 3):
                along_b[f, ob, oa].wait_recv()
                total = total + sums_b[f, ob - 1, oa].astype(jnp.float32)
            if oa == 0:
                own[f] = total
            else:
                send_a[f, oa - 1] = total.astype(jnp.bfloat16)
                along_a[f, oa] = send(
                    send_a.at[f, oa - 1], sums_a.at[f, oa - 1], send6.at[f, oa], recv6.at[f, oa], f, oa)
    for f in range(3):
        total = own[f]
        for oa in (2, 1, 3):
            along_a[f, oa].wait_recv()
            total = total + sums_a[f, oa - 1].astype(jnp.float32)
        mix_ref[:, f * 512 : (f + 1) * 512] = total.astype(jnp.bfloat16)

    for name, copies in enumerate((first, second, along_b, along_a, out, back)):
        for key, copy in copies.items():
            if name < 4 or key[1:] != (0, 0):
                copy.wait_send()


def expert_call(expert_in, plans, expert_up, expert_down):
    tokens, width = expert_in.shape
    vmem = pl.BlockSpec(memory_space=pltpu.VMEM)
    hbm = pl.BlockSpec(memory_space=pl.ANY)
    half = lambda *dims: pltpu.VMEM(dims, jnp.bfloat16)
    sems = lambda *dims: pltpu.SemaphoreType.DMA(dims)
    pairs = lambda *dims: [sems(*dims), sems(*dims)]
    return pl.pallas_call(
        expert_kernel,
        name="experts",
        out_shape=jax.ShapeDtypeStruct((tokens, width), jnp.bfloat16),
        in_specs=[vmem, vmem, hbm, hbm],
        out_specs=vmem,
        scratch_shapes=[
            half(*expert_up.shape[1:]),
            half(*expert_down.shape[1:]),
            half(3, 4, 4, tokens, 512),
            half(3, 4, 4, 128, 128),
            half(3, 4, 4, 128, 128),
            half(3, 2, 4, 4, 4, CAP, 512),
            half(2, 4, 4, 4, CAP, width),
            half(2, 4, 4, 4, CAP, width),
            half(3, 2, 4, 4, 4, CAP, 512),
            half(3, 4, 4, tokens, 512),
            half(3, 3, 4, tokens, 512),
            half(3, 3, tokens, 512),
            half(3, 3, tokens, 512),
            sems(2), sems(6),
        ]
        + pairs(3, 4) + pairs(3, 4, 4) + pairs(3, 2, 4) + pairs(3, 2, 4) + pairs(3, 4, 4) + pairs(3, 4),
        compiler_params=pltpu.CompilerParams(
            collective_id=1, has_side_effects=True, vmem_limit_bytes=67043328
        ),
    )(expert_in, plans, expert_up[0], expert_down[0])


def results_kernel(*refs):
    count = (len(refs) - 2) // 3
    ins, outs, held = refs[:count], refs[count : 2 * count], refs[2 * count : 3 * count]
    in_sems, out_sems = refs[3 * count :]
    loads = [pltpu.make_async_copy(ins[i], held[i], in_sems.at[i]) for i in range(count)]
    stores = [pltpu.make_async_copy(held[i], outs[i], out_sems.at[i]) for i in range(count)]
    for load in loads:
        load.start()
    for load, store in zip(loads, stores):
        load.wait()
        store.start()
    for store in stores:
        store.wait()


def results_call(*arrays):
    hbm = pl.BlockSpec(memory_space=pl.ANY)
    return pl.pallas_call(
        results_kernel,
        name="results",
        out_shape=tuple(jax.ShapeDtypeStruct(a.shape, a.dtype) for a in arrays),
        in_specs=[hbm] * len(arrays),
        out_specs=(hbm,) * len(arrays),
        scratch_shapes=[pltpu.VMEM(a.shape, a.dtype) for a in arrays]
        + [pltpu.SemaphoreType.DMA((len(arrays),)), pltpu.SemaphoreType.DMA((len(arrays),))],
    )(*arrays)


def shards(tokens, attn_gain, w_qkv, w_out, k_cache, v_cache, cache_len, ffn_gain, routes, route_scores, replica_slot, expert_up, expert_down):
    attended, stream, expert_in, appended, plans = attention_call(
        tokens, attn_gain, w_qkv, w_out, k_cache, v_cache, cache_len, ffn_gain, routes, route_scores, replica_slot
    )
    expert_mix = expert_call(expert_in, plans, expert_up, expert_down)
    return results_call(attended, stream, expert_mix, appended)


def solution(mesh):
    rows2 = P(("req", "seq"), None)
    rows3 = P(("req", "seq"), None, None)
    cache = P("req", "seq", None)
    return jax.shard_map(
        shards,
        mesh=mesh,
        in_specs=(rows2, P(), P(), P(), cache, cache, P("req"), P(), rows2, rows2, rows2, rows3, rows3),
        out_specs=(rows2,) * 4,
        check_vma=False,
    )
```

```python
import functools
import numpy as np
import jax
import jax.numpy as jnp
from jax import lax
from jax.experimental import pallas as pl
from jax.experimental.pallas import tpu as pltpu
from jax.sharding import PartitionSpec as P

HEADS = 24
KV_HEADS = 8
HEAD = 64
CAP = 16
MESH = pl.DeviceIdType.MESH

epsilon = 1e-06
residual_scale = 0.22
score_scale = 0.015625
rope_base = 10000.0
neg_big = -1e30


def shifted(req, dim, off):
    stride = (16, 4, 1)[dim]
    at = (req // stride) % 4
    return req + ((at + off) % 4 - at) * stride


def norm_rows(rows, gain):
    widened = rows.astype(jnp.float32)
    mean_square = jnp.mean(widened * widened, axis=-1, keepdims=True)
    return (widened * lax.rsqrt(mean_square + epsilon) * gain).astype(jnp.bfloat16)


def attention_kernel(
    length_ref, tokens_ref, attn_gain_ref, ffn_gain_ref, freq_ref, routes_ref, scores_ref, replica_ref,
    w_qkv_ref, w_out_ref, k_cache_ref, v_cache_ref,
    attended_ref, stream_ref, expert_in_ref, appended_ref, plans_ref,
    w_qkv, w_out, keys, values, queries, heads_out, plans, weight_sems, cache_sems, send_sems, recv_sems,
    plan_send, plan_recv,
):
    rows, width = tokens_ref.shape
    cache_half = k_cache_ref.shape[0]
    kv_width = KV_HEADS * HEAD
    q_width = HEADS * HEAD
    group = HEADS // KV_HEADS
    req, me = lax.axis_index("req"), lax.axis_index("seq")
    partner = 1 - me

    qkv_chunk = 512
    order = (3, 4, 0, 1, 2)
    weight_copies = []
    for at in order:
        cols = pl.ds(at * qkv_chunk, qkv_chunk)
        copy = pltpu.make_async_copy(w_qkv_ref.at[:, cols], w_qkv.at[:, cols], weight_sems.at[at])
        copy.start()
        weight_copies.append(copy)
    mine = pl.ds(pl.multiple_of(me * cache_half, cache_half), cache_half)
    local_k = pltpu.make_async_copy(k_cache_ref, keys.at[mine], cache_sems.at[0])
    local_v = pltpu.make_async_copy(v_cache_ref, values.at[mine], cache_sems.at[1])
    local_k.start()
    local_v.start()
    out_copy = pltpu.make_async_copy(w_out_ref, w_out, weight_sems.at[5])
    out_copy.start()

    barrier = pltpu.get_barrier_semaphore()
    pl.semaphore_signal(barrier, inc=1, device_id=(req, partner), device_id_type=MESH)
    for dim in range(3):
        for off in range(1, 4):
            pl.semaphore_signal(barrier, inc=1, device_id=(shifted(req, dim, off), me), device_id_type=MESH)
    pl.semaphore_wait(barrier, 10)

    def to_partner(src, dst, at):
        return pltpu.make_async_remote_copy(
            src_ref=src, dst_ref=dst, send_sem=send_sems.at[at], recv_sem=recv_sems.at[at],
            device_id=(req, partner), device_id_type=MESH,
        )

    send_k = to_partner(k_cache_ref, keys.at[mine], 0)
    send_v = to_partner(v_cache_ref, values.at[mine], 1)
    send_k.start()
    send_v.start()

    top = routes_ref.shape[0]
    lanes = lax.broadcasted_iota(jnp.int32, (rows, 128), 1)
    row_ids = lax.broadcasted_iota(jnp.int32, (rows, 128), 0)
    expert_ids = lax.broadcasted_iota(jnp.int32, replica_ref.shape, 0)
    replica = replica_ref[...]
    routes = routes_ref[...]
    slots = []
    hits = jnp.zeros((128, rows), jnp.float32)
    for k in range(top):
        slot = jnp.sum(jnp.where(expert_ids == routes[k : k + 1, :], replica, 0), axis=0, keepdims=True)
        slots.append(slot)
        hits = hits + jnp.where(row_ids == slot, 1.0, 0.0)
    earlier = jnp.where(row_ids < lanes, 1.0, 0.0).astype(jnp.bfloat16)
    before = jnp.dot(hits.astype(jnp.bfloat16), earlier, preferred_element_type=jnp.float32)
    scores = scores_ref[...]
    shares = scores / jnp.sum(scores, axis=0, keepdims=True)
    ranks = [jnp.sum(jnp.where(row_ids == slot, before, 0.0), axis=0, keepdims=True) for slot in slots]
    meta = jnp.concatenate([slot.astype(jnp.float32) for slot in slots] + ranks + [shares, shares], axis=0)
    meta = meta.astype(jnp.bfloat16)
    for f in range(3):
        plans[f, 0, 0] = meta
    plan_copies = []
    for f in range(3):
        for off in range(1, 4):
            copy = pltpu.make_async_remote_copy(
                src_ref=plans.at[f, 0, 0], dst_ref=plans.at[f, 0, 4 - off],
                send_sem=plan_send.at[f, off], recv_sem=plan_recv.at[f, off],
                device_id=(shifted(req, f, off), me), device_id_type=MESH,
            )
            copy.start()
            plan_copies.append(copy)

    normed = norm_rows(tokens_ref[...], attn_gain_ref[...].reshape(1, width))
    length = length_ref[0]
    positions = (length + me * rows + row_ids).astype(jnp.float32)
    angles = positions * freq_ref[...]
    cosine = jnp.cos(angles)
    sine = jnp.sin(angles)
    lower = (lanes % HEAD) < HEAD // 2
    signed_sine = jnp.where(lower, -sine, sine)

    def rotated(tile):
        swapped = jnp.where(lower, pltpu.roll(tile, 128 - HEAD // 2, 1), pltpu.roll(tile, HEAD // 2, 1))
        return (tile * cosine + swapped * signed_sine).astype(jnp.bfloat16)

    own_span = pl.ds(pl.multiple_of(2 * cache_half + me * rows, rows), rows)
    even_half = lanes < HEAD
    for turn, at in enumerate(order):
        weight_copies[turn].wait()
        projected = jnp.dot(
            normed, w_qkv[:, at * qkv_chunk : (at + 1) * qkv_chunk], preferred_element_type=jnp.float32
        )
        if at == 3:
            for tile in range(qkv_chunk // 128):
                new_keys = rotated(projected[:, tile * 128 : (tile + 1) * 128])
                keys[own_span, tile * 128 : (tile + 1) * 128] = new_keys
                appended_ref[:, tile * 128 : (tile + 1) * 128] = new_keys
            send_new_k = to_partner(keys.at[own_span], keys.at[own_span], 2)
            send_new_k.start()
        elif at == 4:
            new_values = projected.astype(jnp.bfloat16)
            values[own_span, :] = new_values
            appended_ref[:, kv_width:] = new_values
            send_new_v = to_partner(values.at[own_span], values.at[own_span], 3)
            send_new_v.start()
        else:
            for tile in range(qkv_chunk // 128):
                turned = rotated(projected[:, tile * 128 : (tile + 1) * 128]).astype(jnp.float32) * score_scale
                other = pltpu.roll(turned, HEAD, 1)
                for half in range(2):
                    head = (at * qkv_chunk // 128 + tile) * 2 + half
                    kv, member = head // group, head % group
                    source = turned if half == kv % 2 else other
                    keep = even_half if kv % 2 == 0 else jnp.logical_not(even_half)
                    queries[kv, member * rows : (member + 1) * rows, :] = jnp.where(keep, source, 0.0).astype(jnp.bfloat16)

    for copy in plan_copies:
        copy.wait()
    plan_copies = []
    for f in range(3):
        for off in range(1, 4):
            copy = pltpu.make_async_remote_copy(
                src_ref=plans.at[f, 0], dst_ref=plans.at[f, 4 - off],
                send_sem=plan_send.at[f, 3 + off], recv_sem=plan_recv.at[f, 3 + off],
                device_id=(shifted(req, (f + 1) % 3, off), me), device_id_type=MESH,
            )
            copy.start()
            plan_copies.append(copy)

    local_k.wait()
    local_v.wait()
    send_k.wait()
    send_v.wait()
    send_new_k.wait()
    send_new_v.wait()
    key_total = 2 * cache_half + 2 * rows
    key_lane = lax.broadcasted_iota(jnp.int32, (1, 2 * cache_half), 1)
    cache_bias = jnp.where(key_lane < length, 0.0, neg_big)
    span_lane = lax.broadcasted_iota(jnp.int32, (rows, 2 * rows), 1)
    span_row = lax.broadcasted_iota(jnp.int32, (rows, 2 * rows), 0) + me * rows
    span_bias = jnp.where(span_lane <= span_row, 0.0, neg_big)
    ones = jnp.ones((key_total, 128), jnp.bfloat16)
    dims = (((1,), (1,)), ((), ()))

    def one_group(kv, _):
        pair = pl.ds(pl.multiple_of((kv // 2) * 128, 128), 128)
        pair_keys = keys[:, pair]
        pair_values = jnp.concatenate([values[:, pair], ones], axis=1)
        for member in range(group):
            q = queries[kv, member * rows : (member + 1) * rows, :]
            s_cache = lax.dot_general(q, pair_keys[: 2 * cache_half], dims, preferred_element_type=jnp.float32) + cache_bias
            s_span = lax.dot_general(q, pair_keys[2 * cache_half :], dims, preferred_element_type=jnp.float32) + span_bias
            best = jnp.maximum(jnp.max(s_cache, axis=1, keepdims=True), jnp.max(s_span, axis=1, keepdims=True))
            w_cache = jnp.exp(s_cache - best).astype(jnp.bfloat16)
            w_span = jnp.exp(s_span - best).astype(jnp.bfloat16)
            summed = jnp.dot(w_cache, pair_values[: 2 * cache_half], preferred_element_type=jnp.float32)
            summed = summed + jnp.dot(w_span, pair_values[2 * cache_half :], preferred_element_type=jnp.float32)
            heads_out[kv, member * rows : (member + 1) * rows, :] = summed[:, :128] / summed[:, 128:]
        return 0

    lax.fori_loop(0, KV_HEADS, one_group, 0)

    for tile in range(q_width // 128):
        parts = []
        for half in range(2):
            head = tile * 2 + half
            kv, member = head // group, head % group
            part = heads_out[kv, member * rows : (member + 1) * rows, :]
            parts.append(part if half == kv % 2 else pltpu.roll(part, HEAD, 1))
        attended_ref[:, tile * 128 : (tile + 1) * 128] = jnp.where(even_half, parts[0], parts[1]).astype(jnp.bfloat16)

    out_copy.wait()
    attended = attended_ref[...]
    chunk = 512
    for at in range(width // chunk):
        cols = slice(at * chunk, (at + 1) * chunk)
        product = jnp.dot(attended, w_out[:, cols], preferred_element_type=jnp.float32)
        stream_ref[:, cols] = (tokens_ref[:, cols].astype(jnp.float32) + residual_scale * product).astype(jnp.bfloat16)
    expert_in_ref[...] = norm_rows(stream_ref[...], ffn_gain_ref[...].reshape(1, width))
    for copy in plan_copies:
        copy.wait()
    plans_ref[...] = plans[...]


def attention_call(tokens, attn_gain, w_qkv, w_out, k_cache, v_cache, cache_len, ffn_gain, routes, route_scores, replica_slot):
    rows, width = tokens.shape
    cache_half = k_cache.shape[1]
    kv_width = KV_HEADS * HEAD
    key_total = 2 * cache_half + 2 * rows
    half = HEAD // 2
    freq = np.float64(rope_base) ** (-(np.arange(128) % half) / half)
    freq = jnp.asarray(freq[None, :], jnp.float32)
    vmem = pl.BlockSpec(memory_space=pltpu.VMEM)
    hbm = pl.BlockSpec(memory_space=pl.ANY)
    shape = lambda *dims: jax.ShapeDtypeStruct(dims, jnp.bfloat16)
    return pl.pallas_call(
        attention_kernel,
        name="attention",
        out_shape=(shape(rows, width), shape(rows, width), shape(rows, width), shape(rows, 2 * kv_width), shape(3, 4, 4, 32, 128)),
        in_specs=[pl.BlockSpec(memory_space=pltpu.SMEM)] + [vmem] * 7 + [hbm] * 4,
        out_specs=(vmem,) * 5,
        scratch_shapes=[
            pltpu.VMEM(w_qkv.shape, jnp.bfloat16),
            pltpu.VMEM(w_out.shape, jnp.bfloat16),
            pltpu.VMEM((key_total, kv_width), jnp.bfloat16),
            pltpu.VMEM((key_total, kv_width), jnp.bfloat16),
            pltpu.VMEM((KV_HEADS, HEADS // KV_HEADS * rows, 128), jnp.bfloat16),
            pltpu.VMEM((KV_HEADS, HEADS // KV_HEADS * rows, 128), jnp.float32),
            pltpu.VMEM((3, 4, 4, 32, 128), jnp.bfloat16),
            pltpu.SemaphoreType.DMA((6,)),
            pltpu.SemaphoreType.DMA((2,)),
            pltpu.SemaphoreType.DMA((4,)),
            pltpu.SemaphoreType.DMA((4,)),
            pltpu.SemaphoreType.DMA((3, 7)),
            pltpu.SemaphoreType.DMA((3, 7)),
        ],
        compiler_params=pltpu.CompilerParams(
            collective_id=0, has_side_effects=True, vmem_limit_bytes=60 * 1024 * 1024
        ),
    )(cache_len, tokens, attn_gain, ffn_gain, freq, routes.T, route_scores.T, replica_slot.T,
      w_qkv, w_out, k_cache[0], v_cache[0])


def source_at(f, oa, ob):
    return (ob, oa) if f == 2 else (oa, ob)


def line_view(ref, crel, f, off):
    cols = pl.ds(f * 512, 512)
    every = slice(None)
    if f == 0:
        return ref.at[crel, every, every, off, every, cols]
    if f == 1:
        return ref.at[crel, off, every, every, every, cols]
    return ref.at[crel, every, off, every, every, cols]


def expert_kernel(
    expert_in_ref, plans_ref, up_ref, down_ref, mix_ref,
    up, down, gathered, pick, weigh, outbox, rows_in, rows_out, inbox, sums, relays_b, sums_b, relays_a, send_a, sums_a,
    weight_sems, local_sems, send1, recv1, send2, recv2, send3, recv3, send4, recv4, send5, recv5, send6, recv6,
):
    tokens = expert_in_ref.shape[0]
    req, me = lax.axis_index("req"), lax.axis_index("seq")
    up_copy = pltpu.make_async_copy(up_ref, up, weight_sems.at[0])
    down_copy = pltpu.make_async_copy(down_ref, down, weight_sems.at[1])
    up_copy.start()
    down_copy.start()

    barrier = pltpu.get_barrier_semaphore()
    pl.semaphore_signal(barrier, inc=1, device_id=(req, 1 - me), device_id_type=MESH)
    for dim in range(3):
        for off in range(1, 4):
            for core in range(2):
                pl.semaphore_signal(barrier, inc=1, device_id=(shifted(req, dim, off), core), device_id_type=MESH)
    pl.semaphore_wait(barrier, 19)

    def send(src, dst, send_sem, recv_sem, dim, off, crel=0):
        core = me if crel == 0 else 1 - me
        copy = pltpu.make_async_remote_copy(
            src_ref=src, dst_ref=dst, send_sem=send_sem, recv_sem=recv_sem,
            device_id=(shifted(req, dim, off), core), device_id_type=MESH,
        )
        copy.start()
        return copy

    half = tokens // 2
    low, high = pl.ds(0, half), pl.ds(half, half)

    def block(f, ob, oa):
        if ob == 0 and oa == 0:
            return expert_in_ref.at[:, pl.ds(f * 512, 512)]
        return gathered.at[f, ob, oa]

    first, second = {}, {}

    def start_second(f, oa):
        b = (f + 1) % 3
        second[f, oa, 0] = send(block(f, 0, oa), gathered.at[f, 3, oa], send2.at[f, oa, 0], recv2.at[f, oa, 0], b, 1)
        second[f, oa, 1] = send(block(f, 0, oa), gathered.at[f, 1, oa], send2.at[f, oa, 1], recv2.at[f, oa, 1], b, 3)

    def forward_second(f, oa):
        b = (f + 1) % 3
        second[f, oa, 0].wait_recv()
        second[f, oa, 2] = send(
            gathered.at[f, 3, oa, low], gathered.at[f, 2, oa, low], send2.at[f, oa, 2], recv2.at[f, oa, 2], b, 1)
        second[f, oa, 1].wait_recv()
        second[f, oa, 3] = send(
            gathered.at[f, 1, oa, high], gathered.at[f, 2, oa, high], send2.at[f, oa, 3], recv2.at[f, oa, 3], b, 3)

    for f in range(3):
        first[f, 0] = send(block(f, 0, 0), gathered.at[f, 0, 3], send1.at[f, 0], recv1.at[f, 0], f, 1)
        first[f, 1] = send(block(f, 0, 0), gathered.at[f, 0, 1], send1.at[f, 1], recv1.at[f, 1], f, 3)
    for f in range(3):
        start_second(f, 0)

    line_row = lax.broadcasted_iota(jnp.int32, (128, 128), 0)
    row_crel, row_off, row_rank = line_row // 64, (line_row // 16) % 4, line_row % 16

    def build(f):
        stride = (16, 4, 1)[(f + 2) % 3]
        at = (req // stride) % 4
        target_req = req + ((at + row_off) % 4 - at) * stride
        target_core = me + row_crel - 2 * me * row_crel
        target = ((2 * target_req + target_core) * CAP + row_rank).astype(jnp.float32)
        for ob in range(4):
            def one(oa, _):
                plan = plans_ref[f, ob, oa].astype(jnp.float32)
                position = plan[:8] * CAP + plan[8:16]
                chosen = jnp.zeros((128, 128), jnp.float32)
                for k in range(8):
                    chosen = jnp.where(target == position[k : k + 1, :], plan[16 + k : 17 + k, :], chosen)
                pick[f, ob, oa] = jnp.where(chosen > 0.0, 1.0, 0.0).astype(jnp.bfloat16)
                weigh[f, ob, oa] = jnp.transpose(chosen).astype(jnp.bfloat16)
                return 0
            lax.fori_loop(0, 4, one, 0)

    def select(f, ob, oa):
        d1, d2 = source_at(f, oa, ob)
        rows = jnp.dot(pick[f, ob, oa], block(f, ob, oa)[...], preferred_element_type=jnp.float32)
        outbox[f, :, :, d1, d2] = rows.astype(jnp.bfloat16).reshape(2, 4, CAP, 512)

    build(0)
    for f in range(3):
        first[f, 0].wait_recv()
        first[f, 2] = send(
            gathered.at[f, 0, 3, low], gathered.at[f, 0, 2, low], send1.at[f, 2], recv1.at[f, 2], f, 1)
        first[f, 1].wait_recv()
        first[f, 3] = send(
            gathered.at[f, 0, 1, high], gathered.at[f, 0, 2, high], send1.at[f, 3], recv1.at[f, 3], f, 3)
    for f in range(3):
        forward_second(f, 0)
        start_second(f, 3)
        start_second(f, 1)
    build(1)
    for f in range(3):
        first[f, 2].wait_recv()
        first[f, 3].wait_recv()
        start_second(f, 2)
    build(2)
    for f in range(3):
        for oa in range(4):
            select(f, 0, oa)
        for ob in (1, 3):
            select(f, ob, 0)
    for oa in (3, 1, 2):
        for f in range(3):
            forward_second(f, oa)
        for f in range(3):
            for ob in (1, 3):
                select(f, ob, oa)
    for oa in (0, 3, 1, 2):
        for f in range(3):
            second[f, oa, 2].wait_recv()
            second[f, oa, 3].wait_recv()
            select(f, 2, oa)

    out, back = {}, {}
    for crel in range(2):
        for off in (2, 1, 3, 0):
            for f in range(3):
                src, dst = outbox.at[f, crel, off], line_view(rows_in, crel, f, (4 - off) % 4)
                if crel == 0 and off == 0:
                    copy = pltpu.make_async_copy(src, dst, local_sems.at[f])
                    copy.start()
                else:
                    copy = send(src, dst, send3.at[f, crel, off], recv3.at[f, crel, off], (f + 2) % 3, off, crel)
                out[f, crel, off] = copy

    up_copy.wait()
    down_copy.wait()
    hidden = down.shape[0]
    for crel in range(2):
        for off in range(4):
            for f in range(3):
                if crel == 0 and off == 0:
                    out[f, crel, off].wait()
                else:
                    out[f, crel, off].wait_recv()

        def experts(oz, _):
            rows = rows_in[crel, oz].reshape(256, rows_in.shape[-1])
            gate = jnp.dot(rows, up[:, :hidden], preferred_element_type=jnp.float32)
            lift = jnp.dot(rows, up[:, hidden:], preferred_element_type=jnp.float32)
            active = (gate / (1.0 + jnp.exp(-gate)) * lift).astype(jnp.bfloat16)
            result = jnp.dot(active, down[...], preferred_element_type=jnp.float32)
            rows_out[crel, oz] = result.astype(jnp.bfloat16).reshape(rows_out.shape[2:])
            return 0

        lax.fori_loop(0, 4, experts, 0)
        for off in (2, 1, 3, 0):
            for f in range(3):
                src, dst = line_view(rows_out, crel, f, off), inbox.at[f, crel, (4 - off) % 4]
                if crel == 0 and off == 0:
                    copy = pltpu.make_async_copy(src, dst, local_sems.at[3 + f])
                    copy.start()
                else:
                    copy = send(src, dst, send4.at[f, crel, off], recv4.at[f, crel, off], (f + 2) % 3, off, crel)
                back[f, crel, off] = copy

    for key, copy in back.items():
        if key[1:] == (0, 0):
            copy.wait()
        else:
            copy.wait_recv()

    def line_sum(f, ob, oa):
        d1, d2 = source_at(f, oa, ob)
        rows = inbox[f, :, :, d1, d2].reshape(128, 512)
        return jnp.dot(weigh[f, ob, oa], rows, preferred_element_type=jnp.float32)

    relay_b, along_b, relay_a, along_a = {}, {}, {}, {}
    for oa in (2, 1, 3, 0):
        for f in range(3):
            sums[f, 2, oa] = line_sum(f, 2, oa).astype(jnp.bfloat16)
            for way, (rows, off) in enumerate(((low, 1), (high, 3))):
                relay_b[f, oa, way] = send(
                    sums.at[f, 2, oa, rows], relays_b.at[f, oa, way],
                    send5.at[f, oa, way], recv5.at[f, oa, way], (f + 1) % 3, off)
    for oa in (2, 1, 3, 0):
        for f in range(3):
            for way, (start, off) in enumerate(((0, 1), (half, 3))):
                part = line_sum(f, off, oa)
                relay_b[f, oa, way].wait_recv()
                passed = relays_b[f, oa, way].astype(jnp.float32)
                other = part[half - start : tokens - start]
                sums[f, off, oa, half - start : tokens - start] = other.astype(jnp.bfloat16)
                sums[f, off, oa, start : start + half] = (part[start : start + half] + passed).astype(jnp.bfloat16)
                along_b[f, oa, way] = send(
                    sums.at[f, off, oa], sums_b.at[f, oa, way],
                    send5.at[f, oa, 2 + way], recv5.at[f, oa, 2 + way], (f + 1) % 3, off)

    def total_b(f, oa):
        total = line_sum(f, 0, oa)
        for way in range(2):
            along_b[f, oa, way].wait_recv()
            total = total + sums_b[f, oa, way].astype(jnp.float32)
        return total

    for f in range(3):
        send_a[f, 2] = total_b(f, 2).astype(jnp.bfloat16)
        for way, (rows, off) in enumerate(((low, 1), (high, 3))):
            relay_a[f, way] = send(
                send_a.at[f, 2, rows], relays_a.at[f, way], send6.at[f, way], recv6.at[f, way], f, off)
    for way, (start, off) in enumerate(((0, 1), (half, 3))):
        for f in range(3):
            part = total_b(f, off)
            relay_a[f, way].wait_recv()
            passed = relays_a[f, way].astype(jnp.float32)
            other = part[half - start : tokens - start]
            send_a[f, off, half - start : tokens - start] = other.astype(jnp.bfloat16)
            send_a[f, off, start : start + half] = (part[start : start + half] + passed).astype(jnp.bfloat16)
            along_a[f, way] = send(
                send_a.at[f, off], sums_a.at[f, way], send6.at[f, 2 + way], recv6.at[f, 2 + way], f, off)
    own = [total_b(f, 0) for f in range(3)]
    for f in range(3):
        total = own[f]
        for way in range(2):
            along_a[f, way].wait_recv()
            total = total + sums_a[f, way].astype(jnp.float32)
        mix_ref[:, f * 512 : (f + 1) * 512] = total.astype(jnp.bfloat16)

    for copies in (first, second, relay_b, along_b, relay_a, along_a, out, back):
        for copy in copies.values():
            if copy.is_remote:
                copy.wait_send()


def expert_call(expert_in, plans, expert_up, expert_down):
    tokens, width = expert_in.shape
    vmem = pl.BlockSpec(memory_space=pltpu.VMEM)
    hbm = pl.BlockSpec(memory_space=pl.ANY)
    half = lambda *dims: pltpu.VMEM(dims, jnp.bfloat16)
    sems = lambda *dims: pltpu.SemaphoreType.DMA(dims)
    pairs = lambda *dims: [sems(*dims), sems(*dims)]
    return pl.pallas_call(
        expert_kernel,
        name="experts",
        out_shape=jax.ShapeDtypeStruct((tokens, width), jnp.bfloat16),
        in_specs=[vmem, vmem, hbm, hbm],
        out_specs=vmem,
        scratch_shapes=[
            half(*expert_up.shape[1:]),
            half(*expert_down.shape[1:]),
            half(3, 4, 4, tokens, 512),
            half(3, 4, 4, 128, 128),
            half(3, 4, 4, 128, 128),
            half(3, 2, 4, 4, 4, CAP, 512),
            half(2, 4, 4, 4, CAP, width),
            half(2, 4, 4, 4, CAP, width),
            half(3, 2, 4, 4, 4, CAP, 512),
            half(3, 4, 4, tokens, 512),
            half(3, 4, 2, tokens // 2, 512),
            half(3, 4, 2, tokens, 512),
            half(3, 2, tokens // 2, 512),
            half(3, 4, tokens, 512),
            half(3, 2, tokens, 512),
            sems(2), sems(6),
        ]
        + pairs(3, 4) + pairs(3, 4, 4) + pairs(3, 2, 4) + pairs(3, 2, 4) + pairs(3, 4, 4) + pairs(3, 4),
        compiler_params=pltpu.CompilerParams(
            collective_id=1, has_side_effects=True, vmem_limit_bytes=67043328
        ),
    )(expert_in, plans, expert_up[0], expert_down[0])


def results_kernel(*refs):
    count = (len(refs) - 2) // 3
    ins, outs, held = refs[:count], refs[count : 2 * count], refs[2 * count : 3 * count]
    in_sems, out_sems = refs[3 * count :]
    loads = [pltpu.make_async_copy(ins[i], held[i], in_sems.at[i]) for i in range(count)]
    stores = [pltpu.make_async_copy(held[i], outs[i], out_sems.at[i]) for i in range(count)]
    for load in loads:
        load.start()
    for load, store in zip(loads, stores):
        load.wait()
        store.start()
    for store in stores:
        store.wait()


def results_call(*arrays):
    hbm = pl.BlockSpec(memory_space=pl.ANY)
    return pl.pallas_call(
        results_kernel,
        name="results",
        out_shape=tuple(jax.ShapeDtypeStruct(a.shape, a.dtype) for a in arrays),
        in_specs=[hbm] * len(arrays),
        out_specs=(hbm,) * len(arrays),
        scratch_shapes=[pltpu.VMEM(a.shape, a.dtype) for a in arrays]
        + [pltpu.SemaphoreType.DMA((len(arrays),)), pltpu.SemaphoreType.DMA((len(arrays),))],
    )(*arrays)


def shards(tokens, attn_gain, w_qkv, w_out, k_cache, v_cache, cache_len, ffn_gain, routes, route_scores, replica_slot, expert_up, expert_down):
    attended, stream, expert_in, appended, plans = attention_call(
        tokens, attn_gain, w_qkv, w_out, k_cache, v_cache, cache_len, ffn_gain, routes, route_scores, replica_slot
    )
    expert_mix = expert_call(expert_in, plans, expert_up, expert_down)
    return results_call(attended, stream, expert_mix, appended)


def solution(mesh):
    rows2 = P(("req", "seq"), None)
    rows3 = P(("req", "seq"), None, None)
    cache = P("req", "seq", None)
    return jax.shard_map(
        shards,
        mesh=mesh,
        in_specs=(rows2, P(), P(), P(), cache, cache, P("req"), P(), rows2, rows2, rows2, rows3, rows3),
        out_specs=(rows2,) * 4,
        check_vma=False,
    )
```
